128 devices in a mesh: site: 8 (over x, z_lo), bond: 16 (over z_hi, y, core).
Axes of the slice: x: 4, y: 4, z: 4 (z_hi: 2, z_lo: 2; z = z_hi * 2 + z_lo), core: 2. Of those that a mesh axis runs over, the one named last changes fastest.
Arguments:
- sites: bfloat16 [16, 1024, 2048], P('site', 'bond'), may hold values from -0.1875 to 0.1875
- proj_left: bfloat16 [8, 1024, 2048], P('site', 'bond'), may hold values from -4.1875 to 4.1875
- proj_right: bfloat16 [8, 1024, 2048], P('site', 'bond'), may hold values from -4.1875 to 4.1875
- edge_right: bfloat16 [1024, 2048], P('bond'), may hold values from -4.1875 to 4.1875
- bulk_first: bfloat16 [1024, 2048], P('bond'), may hold values from -0.1875 to 0.1875
- bulk_second: bfloat16 [1024, 2048], P('bond'), may hold values from -0.1875 to 0.1875
- bulk_left_proj: bfloat16 [1024, 2048], P('bond'), may hold values from -4.1875 to 4.1875
- bulk_right_proj: bfloat16 [1024, 2048], P('bond'), may hold values from -4.1875 to 4.1875
- gate: float32 [4, 4], replicated, may hold values from -3 to 3
- gate_mask: int32 [8], P('site'), may hold values 0 or 1
- bond_dims: int32 [8], P('site'), may hold values from 512 to 1024
Outputs:
- new_sites: bfloat16 [16, 1024, 2048], P('site', 'bond')
- new_bulk_first: bfloat16 [1024, 2048], P('bond')
- new_bulk_second: bfloat16 [1024, 2048], P('bond')
The draws below stay inside these ranges and needn't reach their ends.
All inputs are finite; a program needn't handle non-finite values. No bound on the sum of `gate_mask` on one device may be relied on, other than what follows from the above.
Results may differ from the reference program's by a relative error of at most 0.0049.
Values may be sent and summed in bfloat16 or wider, within the bound.
No kernel may reach another device: no remote copies, remote signals or barrier semaphores. Data moves between devices by JAX's collectives and lax.ppermute only.
A program may use at most 128 MiB of HBM per device.

```python
import jax
import jax.numpy as jnp
from jax import lax

CHI = 1024
NS = 16
NP = 8


def set_ends(entries, stream_key, low, high):
    dims = entries.shape
    index_at = [jax.random.randint(jax.random.fold_in(stream_key, axis), (), 0, dims[axis]) for axis in range(len(dims))]
    entries = entries.at[tuple(index_at)].set(low)
    longest = dims.index(max(dims))
    index_at[longest] = (index_at[longest] + 1) % dims[longest]
    return entries.at[tuple(index_at)].set(high)


def steps_of(rng, shape, split, smallest, largest):
    level, own = 1.0, jax.random.fold_in(rng, 6)
    for dim, blocks in split:
        draws = jnp.exp(jax.random.uniform(jax.random.fold_in(own, dim), (blocks,), jnp.float32, smallest / len(split), largest / len(split)))
        level = level * jnp.repeat(draws, shape[dim] // blocks).reshape([-1 if axis == dim else 1 for axis in range(len(shape))])
    return level


def normal_values(own_key, extent, width, reach, shards=(), held_as=jnp.bfloat16):
    loudness = steps_of(own_key, extent, shards, -0.22, 0.18) if shards else 1.0
    values = jax.random.normal(own_key, extent, jnp.float32) * width * loudness
    return jnp.minimum(jnp.maximum(values, -reach), reach).astype(held_as)


def setup_inputs(seed: int = 0) -> dict:
    keys = jax.random.split(jax.random.key(seed), 12)
    return {
        "sites": normal_values(keys[0], (NS, CHI, 2 * CHI), CHI ** -0.5, 0.1875, ((0, 8), (1, 16))),
        "proj_left": normal_values(keys[1], (NP, CHI, 2 * CHI), 0.7, 4.1875, ((0, 8), (1, 16))),
        "proj_right": normal_values(keys[2], (NP, CHI, 2 * CHI), 0.7, 4.1875, ((0, 8), (1, 16))),
        "edge_right": normal_values(keys[3], (CHI, 2 * CHI), 0.7, 4.1875, ((0, 16),)),
        "bulk_first": normal_values(keys[4], (CHI, 2 * CHI), CHI ** -0.5, 0.1875, ((0, 16),)),
        "bulk_second": normal_values(keys[5], (CHI, 2 * CHI), CHI ** -0.5, 0.1875, ((0, 16),)),
        "bulk_left_proj": normal_values(keys[6], (CHI, 2 * CHI), 0.7, 4.1875, ((0, 16),)),
        "bulk_right_proj": normal_values(keys[7], (CHI, 2 * CHI), 0.7, 4.1875, ((0, 16),)),
        "gate": normal_values(keys[8], (4, 4), 0.5, 3.0, (), jnp.float32),
        "gate_mask": set_ends((jax.random.randint(keys[9], (NP,), 0, 2) < 1).astype(jnp.int32), jax.random.fold_in(keys[9], 1), 0, 1),
        "bond_dims": set_ends(jax.random.randint(keys[10], (NP,), CHI // 2, CHI + 1), jax.random.fold_in(keys[10], 1), CHI // 2, CHI).astype(jnp.int32),
    }


def make_theta(left_site, right_site, mixer):
    raw = jnp.stack([jnp.dot(left_site[:, s * CHI:(s + 1) * CHI], right_site, preferred_element_type=jnp.float32) for s in range(2)], axis=1)
    raw = raw.reshape(CHI, 4, CHI)
    mixed = jnp.einsum("xy,ayc->axc", mixer, raw, precision=lax.Precision.HIGHEST)
    return mixed.reshape(CHI, 2, 2 * CHI).astype(jnp.bfloat16)


def project_left(theta, right_proj, keep):
    flat = theta.reshape(2 * CHI, 2 * CHI)
    cols = jnp.dot(flat, right_proj.T, preferred_element_type=jnp.float32).reshape(CHI, 2, CHI)
    return (cols * keep[None, None, :]).reshape(CHI, 2 * CHI).astype(jnp.bfloat16)


def project_right(theta, left_proj, keep):
    flat_proj = left_proj.reshape(CHI, 2, CHI).reshape(2 * CHI, CHI)
    flat = theta.reshape(2 * CHI, 2 * CHI)
    rows = jnp.dot(flat_proj.T, flat, preferred_element_type=jnp.float32)
    return (rows * keep[:, None]).astype(jnp.bfloat16)


def reference(sites, proj_left, proj_right, edge_right, bulk_first, bulk_second, bulk_left_proj, bulk_right_proj, gate, gate_mask, bond_dims):
    identity = jnp.eye(4, dtype=jnp.float32)
    ones = jnp.ones((CHI,), jnp.float32)
    positions = jnp.arange(CHI, dtype=jnp.int32)
    result = [None] * NS
    for pair in range(NP):
        weight = gate_mask[pair].astype(jnp.float32)
        mixer = weight * gate + (1.0 - weight) * identity
        keep = (positions < bond_dims[pair]).astype(jnp.float32)
        left_site = bulk_second if pair == 0 else sites[2 * pair - 1]
        theta = make_theta(left_site, sites[2 * pair], mixer)
        result[2 * pair] = project_right(theta, proj_left[pair], keep)
        if pair > 0:
            result[2 * pair - 1] = project_left(theta, proj_right[pair], keep)
    theta_edge = make_theta(sites[NS - 1], bulk_first, gate)
    result[NS - 1] = project_left(theta_edge, edge_right, ones)
    theta_bulk = make_theta(bulk_second, bulk_first, gate)
    new_bulk_second = project_left(theta_bulk, bulk_right_proj, ones)
    new_bulk_first = project_right(theta_bulk, bulk_left_proj, ones)
    return jnp.stack(result), new_bulk_first, new_bulk_second
```

```python
import jax
import jax.numpy as jnp
from jax import lax
from jax.sharding import Mesh
from jax.sharding import PartitionSpec as P

SITE = ("x", "zl")
BOND = ("zh", "y", "c")
F32 = jnp.float32
BF16 = jnp.bfloat16


def dot(a, b, dims):
    return lax.dot_general(a, b, (dims, ((), ())), preferred_element_type=F32)


def swap(v, axis):
    return lax.ppermute(v, axis, [(0, 1), (1, 0)])


def both(first, own, other):
    return jnp.concatenate(
        [jnp.where(first, own, other), jnp.where(first, other, own)], axis=0
    )


def pick(v, part, parts, index):
    half = v.shape[1] // 2
    size = half // parts
    return jnp.concatenate(
        [v[:, t * half + index * size : t * half + (index + 1) * size] for t in range(2)], axis=1
    )


def mix(mixer, raw, size):
    piece = [raw[y // 2][:, (y % 2) * size : (y % 2 + 1) * size] for y in range(4)]
    out = []
    for s in range(2):
        cols = []
        for t in range(2):
            row = 2 * s + t
            cols.append(sum(mixer[row, y] * piece[y] for y in range(4)))
        out.append(jnp.concatenate(cols, axis=1).astype(BF16))
    return out


def per_device(
    sites,
    proj_left,
    proj_right,
    edge_right,
    bulk_first,
    bulk_second,
    bulk_left_proj,
    bulk_right_proj,
    gate,
    gate_mask,
    bond_dims,
):
    block = sites.shape[1]
    width = sites.shape[2] // 2
    quarter = width // 4
    groups = lax.axis_size(SITE)
    ny = lax.axis_size("y")
    here = lax.axis_index(SITE)
    zh, y, c = (lax.axis_index(name) for name in BOND)
    row_index = lax.axis_index(BOND)
    z0, c0 = zh == 0, c == 0
    first_group = here == 0
    identity = jnp.eye(4, dtype=F32)
    weight = gate_mask[0].astype(F32)
    mixer = weight * gate + (1.0 - weight) * identity
    mixer_left = jnp.where(first_group, gate, mixer)
    positions = jnp.arange(width, dtype=jnp.int32)
    keep = (positions < bond_dims[0]).astype(F32)
    keep_left = jnp.where(first_group, 1.0, keep)

    last_site = sites[sites.shape[0] - 1]
    around = [(g, (g + 1) % groups) for g in range(groups)]
    x_own = lax.ppermute(last_site, SITE, around)
    x_far = lax.ppermute(
        last_site,
        SITE + ("zh",),
        [(2 * g + h, 2 * ((g + 1) % groups) + 1 - h) for g in range(groups) for h in range(2)],
    )
    x_rows = jnp.concatenate([x_own, x_far], axis=0)
    x_left = jnp.concatenate([x_rows, swap(x_rows, "c")], axis=0)
    b_far = lax.ppermute(bulk_second, SITE + ("zh",), [(0, 1), (1, 0)])
    b_rows = jnp.concatenate([bulk_second, b_far], axis=0)
    b_all = jnp.concatenate(
        [b_rows, lax.ppermute(b_rows, SITE + ("c",), [(0, 1), (1, 0)])], axis=0
    )
    x_right = jnp.where(first_group, b_all, x_left)
    l_rows = jnp.concatenate([proj_left[0], swap(proj_left[0], "zh")], axis=0)
    l_all = jnp.concatenate([l_rows, swap(l_rows, "c")], axis=0)

    right_proj = jnp.where(first_group, edge_right, proj_right[0])
    wide = jnp.concatenate([sites[0], right_proj], axis=0)

    def core_stage(v, send):
        even = jnp.concatenate([v[:, q * quarter : (q + 1) * quarter] for q in range(0, 8, 2)], axis=1)
        odd = jnp.concatenate([v[:, q * quarter : (q + 1) * quarter] for q in range(1, 8, 2)], axis=1)
        return both(c0, jnp.where(c0, even, odd), send(jnp.where(c0, odd, even)))

    def z_stage(v, send):
        low, high = pick(v, 0, 2, 0), pick(v, 0, 2, 1)
        return both(z0, jnp.where(z0, low, high), send(jnp.where(z0, high, low)))

    part = z_stage(core_stage(wide, lambda v: swap(v, "c")), lambda v: swap(v, "zh"))
    first_pair = [(0, 1), (1, 0)]
    part_edge = z_stage(
        core_stage(bulk_first, lambda v: lax.ppermute(v, SITE + ("c",), first_pair)),
        lambda v: lax.ppermute(v, SITE + ("zh",), first_pair),
    )
    share = width // groups

    def own_share(v):
        return jnp.concatenate(
            [lax.dynamic_slice_in_dim(v, t * width + here * share, share, 1) for t in range(2)],
            axis=1,
        )

    thin = jnp.concatenate([own_share(bulk_first), own_share(bulk_right_proj)], axis=1)
    thin = both(z0, thin, swap(thin, "zh"))

    rows = part.shape[0]
    message = jnp.concatenate([part, thin], axis=0)
    copies = jnp.broadcast_to(message, (ny, *message.shape))
    got = lax.all_to_all(copies, "y", split_axis=0, concat_axis=0, tiled=True)
    grid = got[:, :rows].reshape(ny, 2, 2, 2, block, 2 * quarter)
    y_all, r_all = (
        grid[:, :, :, k].transpose(1, 0, 2, 3, 4).reshape(4 * ny * block, 2 * quarter)
        for k in range(2)
    )
    thin_own = got[:, rows:]
    thin_far = swap(thin_own, "c")
    thin_all = jnp.stack([jnp.where(c0, thin_own, thin_far), jnp.where(c0, thin_far, thin_own)])
    thin_all = thin_all.reshape(2, ny, 2, block, 4 * share).transpose(2, 1, 0, 3, 4)
    thin_all = thin_all.reshape(4 * ny * block, 4 * share)
    yb_all, rb_all = thin_all[:, : 2 * share], thin_all[:, 2 * share :]

    edge_parts = [part_edge]
    for d in range(1, ny):
        edge_parts.append(lax.ppermute(part_edge, SITE + ("y",), [(k, (k + d) % ny) for k in range(ny)]))
    edge_stack = jnp.stack(edge_parts)
    edge_order = jnp.stack(
        [lax.dynamic_index_in_dim(edge_stack, (y - k) % ny, 0, keepdims=False) for k in range(ny)]
    )
    ye_all = edge_order.reshape(ny, 2, 2 * block, 2 * quarter).transpose(1, 0, 2, 3)
    ye_all = ye_all.reshape(4 * ny * block, 2 * quarter)
    y_left = jnp.where(first_group, ye_all, y_all)

    def theta_of(left, right, mixer, size):
        raw = [dot(left[:, s * width : (s + 1) * width], right, ((1,), (0,))) for s in range(2)]
        return mix(mixer, raw, size)

    theta_right = theta_of(x_right, y_all, mixer, quarter)
    theta_left = theta_of(x_left, y_left, mixer_left, quarter)
    theta_bulk = theta_of(bulk_second, yb_all, gate, share)

    left_part = jnp.concatenate([dot(th, r_all, ((1,), (1,))) for th in theta_left], axis=1)
    half = 2 * block
    left_sum = left_part[:half] + swap(left_part[half:], "c")
    left_far = swap(left_sum[block:].astype(BF16), "zh")
    left_new = (left_sum[:block] + left_far.astype(F32)) * jnp.concatenate([keep_left, keep_left])
    left_new = left_new.astype(BF16)
    returned = lax.ppermute(left_new, SITE, [(b, a) for a, b in around])

    bulk_left = jnp.concatenate([dot(th, rb_all, ((1,), (1,))) for th in theta_bulk], axis=1)
    piece = 2 * width // groups
    bulk_left = jnp.stack([bulk_left[:, k * piece : (k + 1) * piece] for k in range(groups)])
    bulk_left = lax.all_to_all(
        bulk_left.astype(BF16), SITE, split_axis=0, concat_axis=0, tiled=True
    )
    bulk_left = bulk_left.astype(F32).sum(0).astype(BF16)

    right_part = dot(
        jnp.concatenate([l_all[:, :width], l_all[:, width:]], axis=0),
        jnp.concatenate(theta_right, axis=0),
        ((0,), (0,)),
    )
    right_part = right_part.reshape(2, ny, 2 * block, 2 * quarter).transpose(1, 0, 2, 3)
    right_part = right_part.reshape(ny, 4 * block, 2 * quarter).astype(BF16)
    thin_part = sum(
        dot(bulk_left_proj[:, s * width : (s + 1) * width], theta_bulk[s], ((0,), (0,)))
        for s in range(2)
    )
    thin_part = thin_part.reshape(2 * ny, 2, block, 2 * share)
    thin_sum = jnp.where(c0, thin_part[:, 0], thin_part[:, 1])
    thin_sum = thin_sum + swap(jnp.where(c0, thin_part[:, 1], thin_part[:, 0]), "c")
    thin_sum = thin_sum.reshape(2, ny, block, 2 * share).transpose(1, 0, 2, 3)
    thin_sum = jnp.concatenate([thin_sum[:, 0], thin_sum[:, 1]], axis=2).astype(BF16)
    message = jnp.concatenate([right_part, thin_sum], axis=1)
    got = lax.all_to_all(message, "y", split_axis=0, concat_axis=0, tiled=True)
    got = got.astype(F32).sum(0)
    total, thin_total = got[: 4 * block], got[4 * block :]
    keep_z = keep.reshape(2, ny, 2 * block)
    keep_rows = lax.dynamic_index_in_dim(keep_z, y, 1, keepdims=False).reshape(4 * block)
    total = (total * keep_rows[:, None]).astype(BF16)
    low, high = total[:half], total[half:]
    own = jnp.where(z0, low, high)
    far = swap(jnp.where(z0, high, low), "zh")
    pair = jnp.concatenate([jnp.where(z0, own, far), jnp.where(z0, far, own)], axis=1)
    low, high = pair[:block], pair[block:]
    own = jnp.where(c0, low, high)
    far = swap(jnp.where(c0, high, low), "c")
    at = [jnp.where(c0, own, far), jnp.where(c0, far, own)]
    right_new = jnp.concatenate(
        [
            at[k][:, (2 * h + t) * quarter : (2 * h + t + 1) * quarter]
            for t in range(2)
            for h in range(2)
            for k in range(2)
        ],
        axis=1,
    )

    low, high = thin_total[:, : 2 * share], thin_total[:, 2 * share :]
    far = swap(jnp.where(z0, high, low).astype(BF16), "zh")
    bulk_right = (jnp.where(z0, low, high) + far.astype(F32)).astype(BF16)

    ends = jnp.concatenate([bulk_left, bulk_right], axis=1)
    ends = jnp.broadcast_to(ends, (groups, *ends.shape))
    ends = lax.all_to_all(ends, SITE, split_axis=0, concat_axis=0, tiled=True)
    new_second = jnp.concatenate([ends[k, :, :piece] for k in range(groups)], axis=1)
    new_first = jnp.concatenate(
        [
            ends[k, :, piece + t * share : piece + (t + 1) * share]
            for t in range(2)
            for k in range(groups)
        ],
        axis=1,
    )
    return jnp.stack([right_new, returned]), new_first, new_second


def solution(mesh):
    finer = Mesh(mesh.devices.reshape(4, 2, 2, 4, 2), SITE + BOND)
    rows = P(BOND, None)
    stacked = P(SITE, BOND, None)
    placed = (stacked,) * 3 + (rows,) * 5 + (P(), P(SITE), P(SITE))
    return jax.shard_map(
        per_device,
        mesh=finer,
        in_specs=placed,
        out_specs=(stacked, rows, rows),
        check_vma=False,
    )
```

```python
import jax
import jax.numpy as jnp
from jax import lax
from jax.experimental import pallas as pl
from jax.experimental.pallas import tpu as pltpu
from jax.sharding import Mesh
from jax.sharding import PartitionSpec as P

SITE = ("x", "zl")
BOND = ("zh", "y", "c")
F32 = jnp.float32
BF16 = jnp.bfloat16


def dot(a, b, dims):
    return lax.dot_general(a, b, (dims, ((), ())), preferred_element_type=F32)


def swap(v, axis):
    return lax.ppermute(v, axis, [(0, 1), (1, 0)])


def bonds_kernel(
    meta, h, a_ref, p0, p1, p2, left_ref, left_b_ref, keep_ref, send_ref, ys, raw, th, th_b, tmp
):
    c, zh, first, g = meta[0], meta[1], meta[2], meta[3]
    ny, block = 4, 64
    width, cols = 1024, 512
    rows = ny * block

    for zp in range(2):
        for cp in range(2):
            for y in range(ny):
                z_of = lax.rem(zh + zp, 2)
                c_of = lax.rem(c + cp, 2)
                at = pl.multiple_of((z_of * 8 + y * 2 + c_of) * block, block)
                if cp == 0:
                    piece = (p0 if zp == 0 else p1)[y * block : (y + 1) * block, :]
                else:
                    piece = p2[zp * rows + y * block : zp * rows + (y + 1) * block, :]
                ys[pl.ds(at, block), :] = piece

    def theta(x_at, y_at, base, out):
        y_at = pl.multiple_of(y_at, 128)
        for s0 in range(2):
            x_from = pl.multiple_of(x_at + s0 * width, 128)
            raw[s0] = dot(a_ref[:, pl.ds(x_from, width)], ys[:, pl.ds(y_at, cols)], ((1,), (0,)))
        step = 32
        half = cols // 2

        def chunk(i, _):
            r = pl.ds(pl.multiple_of(i * step, step), step)
            parts = [raw[k // 2, r, (k % 2) * half : (k % 2 + 1) * half] for k in range(4)]
            for s in range(2):
                for t in range(2):
                    row = base + 4 * (2 * s + t)
                    val = h[row] * parts[0]
                    for k in range(1, 4):
                        val = val + h[row + k] * parts[k]
                    out[s, r, t * half : (t + 1) * half] = val.astype(out.dtype)
            return 0

        lax.fori_loop(0, rows // step, chunk, 0)

    theta(0, first * cols, 0, th)

    def left_chunk(n, _):
        k_at = pl.multiple_of(n * 256, 256)
        r_part = ys[pl.ds(k_at, 256), 2 * cols : 3 * cols]
        for s in range(2):
            part = dot(th[s], r_part, ((1,), (1,)))
            left_ref[:, pl.ds(pl.multiple_of(s * width + n * 256, 256), 256)] = part.astype(BF16)
        return 0

    lax.fori_loop(0, 4, left_chunk, 0)

    theta(first * (4 * width), 0, 16, th)

    def right_chunk(n, _):
        for s in range(2):
            l_part = a_ref[:, pl.ds(pl.multiple_of(2 * width + s * width + n * 256, 256), 256)]
            part = dot(l_part, th[s], ((0,), (0,)))
            tmp[...] = part if s == 0 else tmp[...] + part
        for j in range(2):
            at = 2 * n + j
            z_of = lax.rem(lax.div(at, ny) + zh, 2)
            y_of = lax.rem(at, ny)
            own = pl.multiple_of(j * 128 + c * block, block)
            far = pl.multiple_of(j * 128 + (1 - c) * block, block)
            keep_ref[z_of, y_of, 0:block, :] = tmp[pl.ds(own, block), :]
            send_ref[z_of, y_of, 0:block, :] = tmp[pl.ds(far, block), :]
        return 0

    lax.fori_loop(0, 4, right_chunk, 0)

    theta(4 * width, cols, 32, th_b)
    picked = [
        th_b[s, pl.ds(pl.multiple_of(y * block + g * 8, 8), 8), :] for s in range(2) for y in range(ny)
    ]
    picked = jnp.concatenate(picked, axis=0).astype(BF16)
    for n in range(4):
        part = dot(picked, ys[n * 256 : (n + 1) * 256, 3 * cols : 4 * cols], ((1,), (1,)))
        for s in range(2):
            left_b_ref[:, s * width + n * 256 : s * width + (n + 1) * 256] = part[
                s * 32 : (s + 1) * 32
            ]
    part = None
    for s in range(2):
        l_part = a_ref[:, 6 * width + s * 128 : 6 * width + (s + 1) * 128]
        one = dot(l_part, th_b[s].astype(BF16), ((0,), (0,)))
        part = one if s == 0 else part + one
    tmp[0:128, :] = part
    for at in range(2 * ny):
        z_of = lax.rem(at // ny + zh, 2)
        own = pl.multiple_of(at * 16 + c * 8, 8)
        far = pl.multiple_of(at * 16 + (1 - c) * 8, 8)
        keep_ref[z_of, at % ny, block : block + 8, :] = tmp[pl.ds(own, 8), :]
        send_ref[z_of, at % ny, block : block + 8, :] = tmp[pl.ds(far, 8), :]


def bonds(meta, h, a, p0, p1, p2):
    smem = pl.BlockSpec(memory_space=pltpu.SMEM)
    vmem = pl.BlockSpec(memory_space=pltpu.VMEM)
    sums = jax.ShapeDtypeStruct((2, 4, 72, 512), F32)
    return pl.pallas_call(
        bonds_kernel,
        out_shape=(
            jax.ShapeDtypeStruct((256, 2048), BF16),
            jax.ShapeDtypeStruct((32, 2048), F32),
            sums,
            sums,
        ),
        in_specs=[smem, smem, vmem, vmem, vmem, vmem],
        out_specs=(vmem, vmem, vmem, vmem),
        scratch_shapes=[
            pltpu.VMEM((1024, 2048), BF16),
            pltpu.VMEM((2, 256, 512), F32),
            pltpu.VMEM((2, 256, 512), BF16),
            pltpu.VMEM((2, 256, 512), F32),
            pltpu.VMEM((256, 512), F32),
        ],
        compiler_params=pltpu.CompilerParams(vmem_limit_bytes=40 * 1024 * 1024),
        cost_estimate=pl.CostEstimate(
            flops=4_000_000_000, bytes_accessed=16_000_000, transcendentals=0
        ),
    )(meta, h, a, p0, p1, p2)


def per_device(
    sites,
    proj_left,
    proj_right,
    edge_right,
    bulk_first,
    bulk_second,
    bulk_left_proj,
    bulk_right_proj,
    gate,
    gate_mask,
    bond_dims,
):
    block = sites.shape[1]
    width = sites.shape[2] // 2
    groups = lax.axis_size(SITE)
    ny = lax.axis_size("y")
    quarter = width // ny
    here = lax.axis_index(SITE)
    zh, y, c = (lax.axis_index(name) for name in BOND)
    row_index = lax.axis_index(BOND)
    first_group = here == 0
    identity = jnp.eye(4, dtype=F32)
    weight = gate_mask[0].astype(F32)
    mixer = weight * gate + (1.0 - weight) * identity
    mixer_left = jnp.where(first_group, gate, mixer)
    positions = jnp.arange(width, dtype=jnp.int32)
    keep = (positions < bond_dims[0]).astype(F32)
    keep_left = jnp.where(first_group, 1.0, keep)
    around = [(g, (g + 1) % groups) for g in range(groups)]

    x_left = lax.ppermute(sites[sites.shape[0] - 1], SITE, around)

    right_proj = jnp.where(first_group, edge_right, proj_right[0])
    arrays = (sites[0], bulk_first, right_proj, bulk_right_proj)
    quarters = jnp.stack(
        [
            jnp.concatenate(
                [
                    v[:, t * width + q * quarter : t * width + (q + 1) * quarter]
                    for v in arrays
                    for t in range(2)
                ],
                axis=1,
            )
            for q in range(ny)
        ]
    )
    got = lax.all_to_all(quarters, "y", split_axis=0, concat_axis=0, tiled=True)
    p0 = got.reshape(ny * block, 2 * width)
    p1 = swap(p0, "zh")
    p2 = swap(jnp.concatenate([p0, p1], axis=0), "c")

    column = lax.broadcasted_iota(jnp.int32, (width, 128), 1)
    source = (column // 8) * block + here * 8 + column % 8
    chosen = (lax.broadcasted_iota(jnp.int32, (width, 128), 0) == source).astype(BF16)
    thin = [
        dot(bulk_left_proj[:, s * width : (s + 1) * width], chosen, ((1,), (0,))).astype(BF16)
        for s in range(2)
    ]
    message = jnp.concatenate([x_left, proj_left[0], bulk_second, *thin], axis=1)
    copies = jnp.broadcast_to(message, (ny, *message.shape))
    got = lax.all_to_all(copies, "y", split_axis=0, concat_axis=0, tiled=True)
    a_rows = got.reshape(ny * block, message.shape[1])

    meta = jnp.stack([c, zh, first_group.astype(jnp.int32), here]).astype(jnp.int32)
    h = jnp.concatenate([mixer_left.reshape(16), mixer.reshape(16), gate.reshape(16)])
    left, left_b, own, send = bonds(meta, h, a_rows, p0, p1, p2)

    sums = own + swap(send, "c")
    far = swap(sums[1].astype(BF16), "zh")
    keep_rows = lax.dynamic_index_in_dim(
        keep.reshape(2, ny, 2, block), zh, 0, keepdims=False
    )
    keep_rows = lax.dynamic_index_in_dim(keep_rows, c, 1, keepdims=False)
    keep_rows = jnp.concatenate([keep_rows, jnp.ones((ny, 8), F32)], axis=1)
    right = ((sums[0] + far.astype(F32)) * keep_rows[:, :, None]).astype(BF16)
    left = jnp.concatenate(
        [left.reshape(ny, block, 2 * width), left_b.reshape(ny, 8, 2 * width).astype(BF16)], axis=1
    )
    message = jnp.concatenate([left, right], axis=2)
    got = lax.all_to_all(message, "y", split_axis=0, concat_axis=0, tiled=True)
    left = got[:, :, : 2 * width].astype(F32).sum(0)
    left_new = (left[:block] * jnp.concatenate([keep_left, keep_left])).astype(BF16)
    returned = lax.ppermute(left_new, SITE, [(b, a) for a, b in around])
    right = jnp.concatenate(
        [
            got[k, :, 2 * width + t * quarter : 2 * width + (t + 1) * quarter]
            for t in range(2)
            for k in range(ny)
        ],
        axis=1,
    )
    ends = jnp.concatenate([left[block:].astype(BF16), right[block:]], axis=0)
    ends = jnp.broadcast_to(ends, (groups, *ends.shape))
    ends = lax.all_to_all(ends, SITE, split_axis=0, concat_axis=0, tiled=True)
    new_second = ends[:, :8].reshape(block, 2 * width)
    new_first = ends[:, 8:].reshape(block, 2 * width)
    return jnp.stack([right[:block], returned]), new_first, new_second


def solution(mesh):
    finer = Mesh(mesh.devices.reshape(4, 2, 2, 4, 2), SITE + BOND)
    rows = P(BOND, None)
    stacked = P(SITE, BOND, None)
    placed = (stacked,) * 3 + (rows,) * 5 + (P(), P(SITE), P(SITE))
    return jax.shard_map(
        per_device,
        mesh=finer,
        in_specs=placed,
        out_specs=(stacked, rows, rows),
        check_vma=False,
    )
```

```python
import jax
import jax.numpy as jnp
from jax import lax
from jax.experimental import pallas as pl
from jax.experimental.pallas import tpu as pltpu
from jax.sharding import Mesh
from jax.sharding import PartitionSpec as P

SITE = ("x", "zl")
BOND = ("zh", "y", "c")
F32 = jnp.float32
BF16 = jnp.bfloat16


def dot(a, b, dims):
    return lax.dot_general(a, b, (dims, ((), ())), preferred_element_type=F32)


def swap(v, axis):
    return lax.ppermute(v, axis, [(0, 1), (1, 0)])


def split_kernel(meta, site, edge, proj, bulk, bulk_proj, bulk_left, out_ref, chosen_ref):
    first, g = meta[3], meta[4]
    quarter, width = 256, 1024
    for q in range(4):
        for t in range(2):
            cols = slice(t * width + q * quarter, t * width + (q + 1) * quarter)
            to = [slice((2 * k + t) * quarter, (2 * k + t + 1) * quarter) for k in range(4)]
            out_ref[q, :, to[0]] = site[0, :, cols]
            out_ref[q, :, to[1]] = bulk[:, cols]
            out_ref[q, :, to[2]] = jnp.where(first == 1, edge[:, cols], proj[0, :, cols])
            out_ref[q, :, to[3]] = bulk_proj[:, cols]
    column = lax.broadcasted_iota(jnp.int32, (width, 128), 1)
    source = (column // 8) * 64 + g * 8 + column % 8
    chosen = jnp.where(lax.broadcasted_iota(jnp.int32, (width, 128), 0) == source, 1.0, 0.0)
    chosen = chosen.astype(BF16)
    for s in range(2):
        part = dot(bulk_left[:, s * width : (s + 1) * width], chosen, ((1,), (0,)))
        chosen_ref[:, s * 128 : (s + 1) * 128] = part.astype(BF16)


def split(meta, sites, edge, proj, bulk, bulk_proj, bulk_left):
    smem = pl.BlockSpec(memory_space=pltpu.SMEM)
    vmem = pl.BlockSpec(memory_space=pltpu.VMEM)
    one = pl.BlockSpec((1, 64, 2048), lambda i: (0, 0, 0))
    flat = pl.BlockSpec((64, 2048), lambda i: (0, 0))
    return pl.pallas_call(
        split_kernel,
        grid=(1,),
        out_shape=(
            jax.ShapeDtypeStruct((4, 64, 2048), BF16),
            jax.ShapeDtypeStruct((64, 256), BF16),
        ),
        in_specs=[smem, one, flat, one, flat, flat, flat],
        out_specs=(
            pl.BlockSpec((4, 64, 2048), lambda i: (0, 0, 0)),
            pl.BlockSpec((64, 256), lambda i: (0, 0)),
        ),
        cost_estimate=pl.CostEstimate(
            flops=40_000_000, bytes_accessed=3_000_000, transcendentals=0
        ),
    )(meta, sites, edge, proj, bulk, bulk_proj, bulk_left)


def bonds_kernel(
    meta, h, own, prev, after, far_low, far_high, p0, p1, p2,
    left_ref, left_b_ref, keep_ref, send_ref, a_ref, ys, raw, th, th_b, tmp,
):
    c, zh, me, first, g = meta[0], meta[1], meta[2], meta[3], meta[4]
    ny, block = 4, 64
    width, cols = 1024, 512
    rows = ny * block
    owner = [lax.rem(me + d, ny) for d in (0, 3, 1, 2)]

    a_ref[0:block, :] = own[...]
    a_ref[block : 2 * block, :] = prev[...]
    a_ref[2 * block : 3 * block, :] = after[...]
    a_ref[3 * block :, 0:3200] = far_low[...]
    a_ref[3 * block :, 3200:6400] = far_high[...]
    for zp in range(2):
        for cp in range(2):
            for y in range(ny):
                z_of = lax.rem(zh + zp, 2)
                c_of = lax.rem(c + cp, 2)
                at = pl.multiple_of((z_of * 8 + y * 2 + c_of) * block, block)
                if cp == 0:
                    piece = (p0 if zp == 0 else p1)[y * block : (y + 1) * block, :]
                else:
                    piece = p2[zp * rows + y * block : zp * rows + (y + 1) * block, :]
                ys[pl.ds(at, block), :] = piece

    def theta(x_at, y_at, base, out):
        y_at = pl.multiple_of(y_at, 128)
        for s0 in range(2):
            x_from = pl.multiple_of(x_at + s0 * width, 128)
            raw[s0] = dot(a_ref[:, pl.ds(x_from, width)], ys[:, pl.ds(y_at, cols)], ((1,), (0,)))
        step = 32
        half = cols // 2

        def chunk(i, _):
            r = pl.ds(pl.multiple_of(i * step, step), step)
            parts = [raw[k // 2, r, (k % 2) * half : (k % 2 + 1) * half] for k in range(4)]
            for s in range(2):
                for t in range(2):
                    row = base + 4 * (2 * s + t)
                    val = h[row] * parts[0]
                    for k in range(1, 4):
                        val = val + h[row + k] * parts[k]
                    out[s, r, t * half : (t + 1) * half] = val.astype(out.dtype)
            return 0

        lax.fori_loop(0, rows // step, chunk, 0)

    theta(0, first * cols, 0, th)

    def left_chunk(n, _):
        k_at = pl.multiple_of(n * 256, 256)
        r_part = ys[pl.ds(k_at, 256), 2 * cols : 3 * cols]
        for s in range(2):
            part = dot(th[s], r_part, ((1,), (1,))).astype(BF16)
            lanes = pl.ds(pl.multiple_of(s * width + n * 256, 256), 256)
            for j in range(ny):
                left_ref[owner[j], :, lanes] = part[j * block : (j + 1) * block]
        return 0

    lax.fori_loop(0, 4, left_chunk, 0)

    theta(first * (4 * width), 0, 16, th)

    def right_chunk(n, _):
        for s in range(2):
            l_part = a_ref[:, pl.ds(pl.multiple_of(2 * width + s * width + n * 256, 256), 256)]
            part = dot(l_part, th[s], ((0,), (0,)))
            tmp[...] = part if s == 0 else tmp[...] + part
        for j in range(2):
            at = 2 * n + j
            z_of = lax.rem(lax.div(at, ny) + zh, 2)
            y_of = lax.rem(at, ny)
            mine = pl.multiple_of(j * 128 + c * block, block)
            other = pl.multiple_of(j * 128 + (1 - c) * block, block)
            keep_ref[z_of, y_of, 0:block, :] = tmp[pl.ds(mine, block), :]
            send_ref[z_of, y_of, 0:block, :] = tmp[pl.ds(other, block), :]
        return 0

    lax.fori_loop(0, 4, right_chunk, 0)

    theta(4 * width, cols, 32, th_b)
    picked = [
        th_b[s, pl.ds(pl.multiple_of(j * block + g * 8, 8), 8), :] for s in range(2) for j in range(ny)
    ]
    picked = jnp.concatenate(picked, axis=0).astype(BF16)
    for n in range(4):
        part = dot(picked, ys[n * 256 : (n + 1) * 256, 3 * cols : 4 * cols], ((1,), (1,)))
        for s in range(2):
            to = (2 * s + n // 2) * 8
            for j in range(ny):
                left_b_ref[owner[j], to : to + 8, (n % 2) * 256 : (n % 2 + 1) * 256] = part[
                    s * 32 + j * 8 : s * 32 + (j + 1) * 8
                ]
    part = None
    for s in range(2):
        l_part = a_ref[:, 6 * width + s * 128 : 6 * width + (s + 1) * 128]
        one = dot(l_part, th_b[s].astype(BF16), ((0,), (0,)))
        part = one if s == 0 else part + one
    tmp[0:128, :] = part
    for at in range(2 * ny):
        z_of = lax.rem(at // ny + zh, 2)
        mine = pl.multiple_of(at * 16 + c * 8, 8)
        other = pl.multiple_of(at * 16 + (1 - c) * 8, 8)
        keep_ref[z_of, at % ny, block : block + 8, :] = tmp[pl.ds(mine, 8), :]
        send_ref[z_of, at % ny, block : block + 8, :] = tmp[pl.ds(other, 8), :]


def bonds(meta, h, *arrays):
    smem = pl.BlockSpec(memory_space=pltpu.SMEM)
    vmem = pl.BlockSpec(memory_space=pltpu.VMEM)
    sums = jax.ShapeDtypeStruct((2, 4, 72, 512), F32)
    return pl.pallas_call(
        bonds_kernel,
        out_shape=(
            jax.ShapeDtypeStruct((4, 64, 2048), BF16),
            jax.ShapeDtypeStruct((4, 32, 512), F32),
            sums,
            sums,
        ),
        in_specs=[smem, smem] + [vmem] * len(arrays),
        out_specs=(vmem, vmem, vmem, vmem),
        scratch_shapes=[
            pltpu.VMEM((256, 6400), BF16),
            pltpu.VMEM((1024, 2048), BF16),
            pltpu.VMEM((2, 256, 512), F32),
            pltpu.VMEM((2, 256, 512), BF16),
            pltpu.VMEM((2, 256, 512), F32),
            pltpu.VMEM((256, 512), F32),
        ],
        compiler_params=pltpu.CompilerParams(vmem_limit_bytes=40 * 1024 * 1024),
        cost_estimate=pl.CostEstimate(
            flops=4_000_000_000, bytes_accessed=16_000_000, transcendentals=0
        ),
    )(meta, h, *arrays)


def per_device(
    sites,
    proj_left,
    proj_right,
    edge_right,
    bulk_first,
    bulk_second,
    bulk_left_proj,
    bulk_right_proj,
    gate,
    gate_mask,
    bond_dims,
):
    block = sites.shape[1]
    width = sites.shape[2] // 2
    groups = lax.axis_size(SITE)
    ny = lax.axis_size("y")
    quarter = width // ny
    here = lax.axis_index(SITE)
    zh, y, c = (lax.axis_index(name) for name in BOND)
    first_group = here == 0
    identity = jnp.eye(4, dtype=F32)
    weight = gate_mask[0].astype(F32)
    mixer = weight * gate + (1.0 - weight) * identity
    mixer_left = jnp.where(first_group, gate, mixer)
    positions = jnp.arange(width, dtype=jnp.int32)
    keep = (positions < bond_dims[0]).astype(F32)
    keep_left = jnp.where(first_group, 1.0, keep)
    around = [(g, (g + 1) % groups) for g in range(groups)]

    meta = jnp.stack([c, zh, y, first_group.astype(jnp.int32), here]).astype(jnp.int32)
    h = jnp.concatenate([mixer_left.reshape(16), mixer.reshape(16), gate.reshape(16)])

    x_left = lax.ppermute(sites[sites.shape[0] - 1], SITE, around)

    quarters, chosen = split(
        meta, sites, edge_right, proj_right, bulk_first, bulk_right_proj, bulk_left_proj
    )
    got = lax.all_to_all(quarters, "y", split_axis=0, concat_axis=0, tiled=True)
    p0 = got.reshape(ny * block, 2 * width)
    p1 = swap(p0, "zh")
    p2 = swap(jnp.concatenate([p0, p1], axis=0), "c")

    up = [(k, (k + 1) % ny) for k in range(ny)]
    down = [(b, a) for a, b in up]
    message = jnp.concatenate([x_left, proj_left[0], bulk_second, chosen], axis=1)
    cut = message.shape[1] // 2
    prev = lax.ppermute(message, "y", up)
    after = lax.ppermute(message, "y", down)
    far_low = lax.ppermute(prev[:, :cut], "y", up)
    far_high = lax.ppermute(after[:, cut:], "y", down)

    left, left_b, own, send = bonds(
        meta, h, message, prev, after, far_low, far_high, p0, p1, p2
    )

    left = lax.all_to_all(left, "y", split_axis=0, concat_axis=0, tiled=True)
    sums = own + swap(send, "c")
    far = swap(sums[1].astype(BF16), "zh")
    left = left.astype(F32).sum(0)
    left_new = (left * jnp.concatenate([keep_left, keep_left])).astype(BF16)
    returned = lax.ppermute(left_new, SITE, [(b, a) for a, b in around])

    keep_rows = lax.dynamic_index_in_dim(
        keep.reshape(2, ny, 2, block), zh, 0, keepdims=False
    )
    keep_rows = lax.dynamic_index_in_dim(keep_rows, c, 1, keepdims=False)
    keep_rows = jnp.concatenate([keep_rows, jnp.ones((ny, 8), F32)], axis=1)
    right = ((sums[0] + far.astype(F32)) * keep_rows[:, :, None]).astype(BF16)
    message = jnp.concatenate([right, left_b.astype(BF16)], axis=1)
    got = lax.all_to_all(message, "y", split_axis=0, concat_axis=0, tiled=True)
    right = jnp.concatenate(
        [
            got[k, : block + 8, t * quarter : (t + 1) * quarter]
            for t in range(2)
            for k in range(ny)
        ],
        axis=1,
    )
    left_b = got[:, block + 8 :].astype(F32).sum(0).astype(BF16)
    left_b = jnp.concatenate([left_b[8 * k : 8 * (k + 1)] for k in range(4)], axis=1)
    ends = jnp.concatenate([left_b, right[block:]], axis=0)
    ends = jnp.broadcast_to(ends, (groups, *ends.shape))
    ends = lax.all_to_all(ends, SITE, split_axis=0, concat_axis=0, tiled=True)
    new_second = ends[:, :8].reshape(block, 2 * width)
    new_first = ends[:, 8:].reshape(block, 2 * width)
    return jnp.stack([right[:block], returned]), new_first, new_second


def solution(mesh):
    finer = Mesh(mesh.devices.reshape(4, 2, 2, 4, 2), SITE + BOND)
    rows = P(BOND, None)
    stacked = P(SITE, BOND, None)
    placed = (stacked,) * 3 + (rows,) * 5 + (P(), P(SITE), P(SITE))
    return jax.shard_map(
        per_device,
        mesh=finer,
        in_specs=placed,
        out_specs=(stacked, rows, rows),
        check_vma=False,
    )
```

```python
import jax
import jax.numpy as jnp
from jax import lax
from jax.experimental import pallas as pl
from jax.experimental.pallas import tpu as pltpu
from jax.sharding import Mesh
from jax.sharding import PartitionSpec as P


SITE = ("x", "zl")
BOND = ("zh", "y", "c")
VMEM_BYTES = 60 * 1024 * 1024
F32 = jnp.float32
BF16 = jnp.bfloat16


def dot(a, b, dims):
    return lax.dot_general(a, b, (dims, ((), ())), preferred_element_type=F32)


def split_kernel(meta, site, edge, proj, bulk, bulk_proj, bulk_left, out_ref, bulk_ref):
    first, g = meta[3], meta[4]
    quarter, width = 256, 1024
    column = lax.broadcasted_iota(jnp.int32, (width, 128), 1)
    source = (column // 8) * 64 + g * 8 + column % 8
    chosen = jnp.where(lax.broadcasted_iota(jnp.int32, (width, 128), 0) == source, 1.0, 0.0)
    chosen = chosen.astype(BF16)
    for s in range(2):
        part = dot(bulk_left[:, s * width : (s + 1) * width], chosen, ((1,), (0,))).astype(BF16)
        for q in range(4):
            bulk_ref[q, :, width + s * 128 : width + (s + 1) * 128] = part
    for q in range(4):
        for t in range(2):
            cols = slice(t * width + q * quarter, t * width + (q + 1) * quarter)
            low = slice(t * quarter, (t + 1) * quarter)
            high = slice((2 + t) * quarter, (3 + t) * quarter)
            out_ref[q, :, low] = site[0, :, cols]
            bulk_ref[q, :, low] = bulk[:, cols]
            out_ref[q, :, high] = jnp.where(first == 1, edge[:, cols], proj[0, :, cols])
            bulk_ref[q, :, high] = bulk_proj[:, cols]


def split(meta, sites, edge, proj, bulk, bulk_proj, bulk_left):
    smem = pl.BlockSpec(memory_space=pltpu.SMEM)
    one = pl.BlockSpec((1, 64, 2048), lambda i: (0, 0, 0))
    flat = pl.BlockSpec((64, 2048), lambda i: (0, 0))
    return pl.pallas_call(
        split_kernel,
        grid=(1,),
        out_shape=(
            jax.ShapeDtypeStruct((4, 64, 1024), BF16),
            jax.ShapeDtypeStruct((4, 64, 1280), BF16),
        ),
        in_specs=[smem, one, flat, one, flat, flat, flat],
        out_specs=(
            pl.BlockSpec((4, 64, 1024), lambda i: (0, 0, 0)),
            pl.BlockSpec((4, 64, 1280), lambda i: (0, 0, 0)),
        ),
        cost_estimate=pl.CostEstimate(
            flops=40_000_000, bytes_accessed=3_000_000, transcendentals=0
        ),
        name="split",
    )(meta, sites, edge, proj, bulk, bulk_proj, bulk_left)


def theta(h, base, x_of, y_part, raw, out):
    for s0 in range(2):
        raw[s0] = dot(x_of(s0), y_part, ((1,), (0,)))
    step, half = 32, 256

    def chunk(i, _):
        r = pl.ds(pl.multiple_of(i * step, step), step)
        parts = [raw[k // 2, r, (k % 2) * half : (k % 2 + 1) * half] for k in range(4)]
        for s in range(2):
            for t in range(2):
                row = base + 4 * (2 * s + t)
                val = h[row] * parts[0]
                for k in range(1, 4):
                    val = val + h[row + k] * parts[k]
                out[s, r, t * half : (t + 1) * half] = val.astype(out.dtype)
        return 0

    lax.fori_loop(0, 256 // step, chunk, 0)


def row_copies(parts, cols, ys, zh, c, sem):
    copies = []
    for n, part in enumerate(parts):
        z_of = lax.rem(zh + n % 2, 2)
        c_of = lax.rem(c + n // 2, 2)
        for y in range(4):
            at = pl.multiple_of((z_of * 8 + y * 2 + c_of) * 64, 64)
            copies.append(
                pltpu.make_async_copy(
                    part.at[y, :, 0:cols], ys.at[pl.ds(at, 64), :], sem.at[n * 4 + y]
                )
            )
    return copies


def bulk_kernel(
    meta, h, own, prev, after, far_low, far_high, b0, b1, b2, b3,
    left_ref, keep_ref, send_ref, xs, ys, ls, raw, th, tmp, sem, sem_y,
):
    c, zh, me, g = meta[0], meta[1], meta[2], meta[4]
    ny, block, width, cols = 4, 64, 1024, 512
    owner = [lax.rem(me + d, ny) for d in (0, 3, 1, 2)]
    rows = [pl.ds(pl.multiple_of(o * block, block), block) for o in owner]
    copies = row_copies((b0, b1, b2, b3), 2 * cols, ys, zh, c, sem_y)
    for n, part in enumerate((own, prev, after)):
        copies.append(pltpu.make_async_copy(part, xs.at[rows[n], :], sem.at[n]))
    copies.append(pltpu.make_async_copy(far_low, xs.at[rows[3], 0:width], sem.at[3]))
    copies.append(pltpu.make_async_copy(far_high, xs.at[rows[3], width : 2 * width], sem.at[4]))
    copies.append(pltpu.make_async_copy(b0.at[:, :, width : width + 256], ls, sem.at[5]))
    for copy in copies:
        copy.start()
    for copy in copies:
        copy.wait()

    theta(h, 32, lambda s: xs[:, s * width : (s + 1) * width], ys[:, 0:cols], raw, th)
    picked = [
        th[s, pl.ds(pl.multiple_of(y * block + g * 8, 8), 8), :] for s in range(2) for y in range(ny)
    ]
    picked = jnp.concatenate(picked, axis=0).astype(BF16)
    for n in range(4):
        part = dot(picked, ys[n * 256 : (n + 1) * 256, cols : 2 * cols], ((1,), (1,)))
        for s in range(2):
            to = (2 * s + n // 2) * 8
            for y in range(ny):
                left_ref[y, to : to + 8, (n % 2) * 256 : (n % 2 + 1) * 256] = part[
                    s * 32 + y * 8 : s * 32 + (y + 1) * 8
                ]
    part = None
    for s in range(2):
        l_part = ls[:, :, s * 128 : (s + 1) * 128].reshape(ny * block, 128)
        one = dot(l_part, th[s].astype(BF16), ((0,), (0,)))
        part = one if s == 0 else part + one
    tmp[...] = part
    for at in range(2 * ny):
        z_of = lax.rem(at // ny + zh, 2)
        mine = pl.multiple_of(at * 16 + c * 8, 8)
        other = pl.multiple_of(at * 16 + (1 - c) * 8, 8)
        keep_ref[z_of, at % ny] = tmp[pl.ds(mine, 8), :]
        send_ref[z_of, at % ny] = tmp[pl.ds(other, 8), :]


def window_kernel(
    meta, h, a_own, a_prev, a_after, x_far, l_far, p0, p1, p2, p3, own, prev, after, far_low, far_high, b0, b1, b2, b3,
    left_ref, keep_ref, send_ref,
    xs, ls, xb, ys, yb, raw, th, tmp, sem, sem_y, sem_b,
):
    c, zh, me, first = meta[0], meta[1], meta[2], meta[3]
    ny, block, width, cols = 4, 64, 1024, 512
    owner = [lax.rem(me + d, ny) for d in (0, 3, 1, 2)]
    rows = [pl.ds(pl.multiple_of(o * block, block), block) for o in owner]
    main = row_copies((p0, p1, p2, p3), 2 * cols, ys, zh, c, sem_y)
    for n, part in enumerate((a_own.at[0], a_prev.at[0], a_after.at[0], x_far)):
        main.append(pltpu.make_async_copy(part, xs.at[rows[n], :], sem.at[n]))
    for n, part in enumerate((own, prev, after)):
        main.append(pltpu.make_async_copy(part, xb.at[rows[n], :], sem.at[4 + n]))
    main.append(pltpu.make_async_copy(far_low, xb.at[rows[3], 0:width], sem.at[7]))
    main.append(pltpu.make_async_copy(far_high, xb.at[rows[3], width : 2 * width], sem.at[8]))
    main += row_copies((b0, b1, b2, b3), cols, yb, zh, c, sem_b)
    later = [
        pltpu.make_async_copy(part, ls.at[rows[n], :], sem.at[10 + n])
        for n, part in enumerate((a_own.at[1], a_prev.at[1], a_after.at[1], l_far))
    ]
    for copy in main + later:
        copy.start()
    for copy in main:
        copy.wait()

    @pl.when(first == 1)
    def _():
        theta(h, 0, lambda s: xs[:, s * width : (s + 1) * width], yb[...], raw, th)

    @pl.when(first == 0)
    def _():
        theta(h, 0, lambda s: xs[:, s * width : (s + 1) * width], ys[:, 0:cols], raw, th)

    def left_chunk(n, _):
        k_at = pl.multiple_of(n * 256, 256)
        r_part = ys[pl.ds(k_at, 256), cols : 2 * cols]
        for s in range(2):
            part = dot(th[s], r_part, ((1,), (1,))).astype(BF16)
            lanes = pl.ds(pl.multiple_of(s * width + n * 256, 256), 256)
            for y in range(ny):
                left_ref[y, :, lanes] = part[y * block : (y + 1) * block]
        return 0

    lax.fori_loop(0, 4, left_chunk, 0)

    @pl.when(first == 1)
    def _():
        theta(h, 16, lambda s: xb[:, s * width : (s + 1) * width], ys[:, 0:cols], raw, th)

    for copy in later:
        copy.wait()

    def right_chunk(n, _):
        part = None
        for s in range(2):
            l_part = ls[:, pl.ds(pl.multiple_of(s * width + n * 256, 256), 256)]
            one = dot(l_part, th[s], ((0,), (0,)))
            part = one if s == 0 else part + one
        tmp[...] = part
        for j in range(2):
            at = 2 * n + j
            z_of = lax.rem(lax.div(at, ny) + zh, 2)
            y_of = lax.rem(at, ny)
            mine = pl.multiple_of(j * 128 + c * block, block)
            other = pl.multiple_of(j * 128 + (1 - c) * block, block)
            keep_ref[z_of, y_of] = tmp[pl.ds(mine, block), :]
            send_ref[z_of, y_of] = tmp[pl.ds(other, block), :]
        return 0

    lax.fori_loop(0, 4, right_chunk, 0)


def call(kernel, outs, scratch, flops, meta, h, *arrays):
    smem = pl.BlockSpec(memory_space=pltpu.SMEM)
    vmem = pl.BlockSpec(memory_space=pltpu.VMEM)
    anywhere = pl.BlockSpec(memory_space=pltpu.HBM)
    return pl.pallas_call(
        kernel,
        out_shape=outs,
        in_specs=[smem, smem] + [anywhere] * len(arrays),
        out_specs=(vmem,) * len(outs),
        scratch_shapes=scratch,
        compiler_params=pltpu.CompilerParams(vmem_limit_bytes=VMEM_BYTES),
        cost_estimate=pl.CostEstimate(
            flops=flops, bytes_accessed=10_000_000, transcendentals=0
        ),
    )(meta, h, *arrays)


def ends_kernel(got, out):
    low = got[:, 8:40, :].astype(F32)
    low = (low[0] + low[1] + low[2] + low[3]).astype(BF16)
    left = jnp.concatenate([low[8 * k : 8 * (k + 1)] for k in range(4)], axis=1)
    right = [got[k, 0:8, t * 256 : (t + 1) * 256] for t in range(2) for k in range(4)]
    ends = jnp.concatenate([left, jnp.concatenate(right, axis=1)], axis=0)
    for g in range(8):
        out[g] = ends


def bulk_ends(got):
    return pl.pallas_call(
        ends_kernel,
        out_shape=jax.ShapeDtypeStruct((8, 16, 2048), BF16),
        cost_estimate=pl.CostEstimate(flops=1_000_000, bytes_accessed=700_000, transcendentals=0),
        name="finish",
    )(got)


def bulk_bond(meta, h, *arrays):
    sums = jax.ShapeDtypeStruct((2, 4, 8, 512), F32)
    return call(
        bulk_kernel,
        (jax.ShapeDtypeStruct((4, 32, 512), F32), sums, sums),
        [
            pltpu.VMEM((256, 2048), BF16),
            pltpu.VMEM((1024, 1024), BF16),
            pltpu.VMEM((4, 64, 256), BF16),
            pltpu.VMEM((2, 256, 512), F32),
            pltpu.VMEM((2, 256, 512), F32),
            pltpu.VMEM((128, 512), F32),
            pltpu.SemaphoreType.DMA((6,)),
            pltpu.SemaphoreType.DMA((16,)),
        ],
        1_000_000_000,
        meta,
        h,
        *arrays,
    )


def window_bonds(meta, h, *arrays):
    sums = jax.ShapeDtypeStruct((2, 4, 64, 512), F32)
    return call(
        window_kernel,
        (jax.ShapeDtypeStruct((4, 64, 2048), BF16), sums, sums),
        [
            pltpu.VMEM((256, 2048), BF16),
            pltpu.VMEM((256, 2048), BF16),
            pltpu.VMEM((256, 2048), BF16),
            pltpu.VMEM((1024, 1024), BF16),
            pltpu.VMEM((1024, 512), BF16),
            pltpu.VMEM((2, 256, 512), F32),
            pltpu.VMEM((2, 256, 512), BF16),
            pltpu.VMEM((256, 512), F32),
            pltpu.SemaphoreType.DMA((14,)),
            pltpu.SemaphoreType.DMA((16,)),
            pltpu.SemaphoreType.DMA((16,)),
        ],
        3_000_000_000,
        meta,
        h,
        *arrays,
    )


def half_step(
    sites,
    proj_left,
    proj_right,
    edge_right,
    bulk_first,
    bulk_second,
    bulk_left_proj,
    bulk_right_proj,
    gate,
    gate_mask,
    bond_dims,
):
    block = sites.shape[1]
    width = sites.shape[2] // 2
    groups = lax.axis_size(SITE)
    ny = lax.axis_size("y")
    quarter = width // ny
    here = lax.axis_index(SITE)
    zh, y, c = (lax.axis_index(name) for name in BOND)
    first_group = here == 0
    identity = jnp.eye(4, dtype=F32)
    weight = gate_mask[0].astype(F32)
    mixer = weight * gate + (1.0 - weight) * identity
    mixer_left = jnp.where(first_group, gate, mixer)
    positions = jnp.arange(width, dtype=jnp.int32)
    keep = (positions < bond_dims[0]).astype(F32)
    keep_left = jnp.where(first_group, 1.0, keep)
    around = [(g, (g + 1) % groups) for g in range(groups)]

    meta = jnp.stack([c, zh, y, first_group.astype(jnp.int32), here]).astype(jnp.int32)
    h = jnp.concatenate([mixer_left.reshape(16), mixer.reshape(16), gate.reshape(16)])
    up = [(k, (k + 1) % ny) for k in range(ny)]
    down = [(b, a) for a, b in up]
    back = [(b, a) for a, b in around]

    def exchange(v, axis):
        return lax.all_to_all(v, axis, split_axis=0, concat_axis=0, tiled=True)

    pair = [(0, 1), (1, 0)]

    x_own = lax.ppermute(sites[sites.shape[0] - 1], SITE, around)
    b_prev = lax.ppermute(bulk_second, "y", up)
    b_after = lax.ppermute(bulk_second, "y", down)

    quarters, bulk_quarters = split(
        meta, sites, edge_right, proj_right, bulk_first, bulk_right_proj, bulk_left_proj
    )
    q0 = exchange(bulk_quarters, "y")
    q1 = lax.ppermute(q0, "zh", pair)
    q2 = lax.ppermute(q0, "c", pair)
    q3 = lax.ppermute(q1, "c", pair)
    b_low = lax.ppermute(b_prev[:, :width], "y", up)
    b_high = lax.ppermute(b_after[:, width:], "y", down)
    p0 = exchange(quarters, "y")
    p1 = lax.ppermute(p0, "zh", pair)
    p2 = lax.ppermute(p0, "c", pair)
    p3 = lax.ppermute(p1, "c", pair)
    a_own = jnp.stack([x_own, proj_left[0]])
    a_prev = lax.ppermute(a_own, "y", up)
    a_after = lax.ppermute(a_own, "y", down)
    x_cut = a_prev[0]
    l_cut = a_after[1]
    x_far = lax.ppermute(x_cut, "y", up)
    l_far = lax.ppermute(l_cut, "y", down)

    bulk_rows = (bulk_second, b_prev, b_after, b_low, b_high)
    bulk_left, bulk_own, bulk_send = bulk_bond(meta, h, *bulk_rows, q0, q1, q2, q3)
    got = lax.ppermute(bulk_send, "c", pair)
    far = lax.ppermute((bulk_own[1] + got[1]).astype(BF16), "zh", pair)
    bulk_right = (bulk_own[0] + got[0] + far.astype(F32)).astype(BF16)
    got = exchange(jnp.concatenate([bulk_right, bulk_left.astype(BF16)], axis=1), "y")
    ends = bulk_ends(got)
    ends = exchange(ends, SITE)
    new_second = ends[:, :8].reshape(block, 2 * width)
    new_first = ends[:, 8:].reshape(block, 2 * width)

    left, right_own, right_send = window_bonds(
        meta, h, a_own, a_prev, a_after, x_far, l_far, p0, p1, p2, p3, *bulk_rows, q0, q1, q2, q3,
    )
    got = lax.ppermute(right_send, "c", pair)
    left = exchange(left, "y")
    far = (right_own[1] + got[1]).astype(BF16)
    far = lax.ppermute(far, "zh", pair)
    keep_rows = lax.dynamic_index_in_dim(
        keep.reshape(2, ny, 2, block), zh, 0, keepdims=False
    )
    keep_rows = lax.dynamic_index_in_dim(keep_rows, c, 1, keepdims=False)
    right = (right_own[0] + got[0] + far.astype(F32)) * keep_rows[:, :, None]
    got = exchange(right.astype(BF16), "y")
    left = left.astype(F32).sum(0) * jnp.concatenate([keep_left, keep_left])
    returned = lax.ppermute(left.astype(BF16), SITE, back)
    right = jnp.concatenate(
        [got[k, :, t * quarter : (t + 1) * quarter] for t in range(2) for k in range(ny)], axis=1
    )
    return jnp.stack([right, returned]), new_first, new_second


def solution(mesh):
    finer = Mesh(mesh.devices.reshape(4, 2, 2, 4, 2), SITE + BOND)
    rows = P(BOND, None)
    stacked = P(SITE, BOND, None)
    placed = (stacked,) * 3 + (rows,) * 5 + (P(), P(SITE), P(SITE))
    return jax.shard_map(
        half_step,
        mesh=finer,
        in_specs=placed,
        out_specs=(stacked, rows, rows),
        check_vma=False,
    )
```

```python
import jax
import jax.numpy as jnp
from jax import lax
from jax.experimental import pallas as pl
from jax.experimental.pallas import tpu as pltpu
from jax.sharding import Mesh
from jax.sharding import PartitionSpec as P


SITE = ("x", "zl")
BOND = ("zh", "y", "c")
VMEM_BYTES = 60 * 1024 * 1024
F32 = jnp.float32
BF16 = jnp.bfloat16


def dot(a, b, dims):
    return lax.dot_general(a, b, (dims, ((), ())), preferred_element_type=F32)


def split_kernel(meta, site, edge, proj, bulk, bulk_proj, bulk_left, out_ref, bulk_ref):
    first, g = meta[3], meta[4]
    quarter, width = 256, 1024
    column = lax.broadcasted_iota(jnp.int32, (width, 128), 1)
    source = (column // 8) * 64 + g * 8 + column % 8
    chosen = jnp.where(lax.broadcasted_iota(jnp.int32, (width, 128), 0) == source, 1.0, 0.0)
    chosen = chosen.astype(BF16)
    for s in range(2):
        part = dot(bulk_left[:, s * width : (s + 1) * width], chosen, ((1,), (0,))).astype(BF16)
        for q in range(4):
            bulk_ref[q, :, width + s * 128 : width + (s + 1) * 128] = part
    for q in range(4):
        for t in range(2):
            cols = slice(t * width + q * quarter, t * width + (q + 1) * quarter)
            low = slice(t * quarter, (t + 1) * quarter)
            high = slice((2 + t) * quarter, (3 + t) * quarter)
            out_ref[q, :, low] = site[0, :, cols]
            bulk_ref[q, :, low] = bulk[:, cols]
            out_ref[q, :, high] = jnp.where(first == 1, edge[:, cols], proj[0, :, cols])
            bulk_ref[q, :, high] = bulk_proj[:, cols]


def split(meta, sites, edge, proj, bulk, bulk_proj, bulk_left):
    smem = pl.BlockSpec(memory_space=pltpu.SMEM)
    one = pl.BlockSpec((1, 64, 2048), lambda i: (0, 0, 0))
    flat = pl.BlockSpec((64, 2048), lambda i: (0, 0))
    return pl.pallas_call(
        split_kernel,
        grid=(1,),
        out_shape=(
            jax.ShapeDtypeStruct((4, 64, 1024), BF16),
            jax.ShapeDtypeStruct((4, 64, 1280), BF16),
        ),
        in_specs=[smem, one, flat, one, flat, flat, flat],
        out_specs=(
            pl.BlockSpec((4, 64, 1024), lambda i: (0, 0, 0)),
            pl.BlockSpec((4, 64, 1280), lambda i: (0, 0, 0)),
        ),
        cost_estimate=pl.CostEstimate(
            flops=40_000_000, bytes_accessed=3_000_000, transcendentals=0
        ),
        name="split",
    )(meta, sites, edge, proj, bulk, bulk_proj, bulk_left)


def theta(h, base, x_of, y_part, raw, out):
    for s0 in range(2):
        raw[s0] = dot(x_of(s0), y_part, ((1,), (0,)))
    step, half = 32, 256

    def chunk(i, _):
        r = pl.ds(pl.multiple_of(i * step, step), step)
        parts = [raw[k // 2, r, (k % 2) * half : (k % 2 + 1) * half] for k in range(4)]
        for s in range(2):
            for t in range(2):
                row = base + 4 * (2 * s + t)
                val = h[row] * parts[0]
                for k in range(1, 4):
                    val = val + h[row + k] * parts[k]
                out[s, r, t * half : (t + 1) * half] = val.astype(out.dtype)
        return 0

    lax.fori_loop(0, 256 // step, chunk, 0)


def row_copies(parts, low, high, ys, zh, c, sem):
    copies = []
    for n, part in enumerate(parts):
        z_of = lax.rem(zh + n % 2, 2)
        c_of = lax.rem(c + n // 2, 2)
        for y in range(4):
            at = pl.multiple_of((z_of * 8 + y * 2 + c_of) * 64, 64)
            copies.append(
                pltpu.make_async_copy(
                    part.at[y, :, low:high], ys.at[pl.ds(at, 64), :], sem.at[n * 4 + y]
                )
            )
    return copies


def bulk_kernel(
    meta, h, own, prev, after, far_low, far_high, b0, b1, b2, b3,
    left_ref, keep_ref, send_ref, xs, ys, ls, raw, th, tmp, left_f32, sem, sem_y,
):
    c, zh, me, g = meta[0], meta[1], meta[2], meta[4]
    ny, block, width, cols = 4, 64, 1024, 512
    owner = [lax.rem(me + d, ny) for d in (0, 3, 1, 2)]
    rows = [pl.ds(pl.multiple_of(o * block, block), block) for o in owner]
    copies = row_copies((b0, b1, b2, b3), 0, 2 * cols, ys, zh, c, sem_y)
    for n, part in enumerate((own, prev, after)):
        copies.append(pltpu.make_async_copy(part, xs.at[rows[n], :], sem.at[n]))
    copies.append(pltpu.make_async_copy(far_low, xs.at[rows[3], 0:width], sem.at[3]))
    copies.append(pltpu.make_async_copy(far_high, xs.at[rows[3], width : 2 * width], sem.at[4]))
    copies.append(pltpu.make_async_copy(b0.at[:, :, width : width + 256], ls, sem.at[5]))
    for copy in copies:
        copy.start()
    for copy in copies:
        copy.wait()

    theta(h, 32, lambda s: xs[:, s * width : (s + 1) * width], ys[:, 0:cols], raw, th)
    picked = [
        th[s, pl.ds(pl.multiple_of(o * block + g * 8, 8), 8), :] for s in range(2) for o in owner
    ]
    picked = jnp.concatenate(picked, axis=0).astype(BF16)
    for n in range(4):
        part = dot(picked, ys[n * 256 : (n + 1) * 256, cols : 2 * cols], ((1,), (1,)))
        for s in range(2):
            for j in range(ny):
                left_f32[j, (4 * s + n) * 8 : (4 * s + n + 1) * 8, :] = part[
                    s * 32 + j * 8 : s * 32 + (j + 1) * 8
                ]
    left_ref[...] = left_f32[...].astype(BF16)
    part = None
    for s in range(2):
        l_part = ls[:, :, s * 128 : (s + 1) * 128].reshape(ny * block, 128)
        one = dot(l_part, th[s].astype(BF16), ((0,), (0,)))
        part = one if s == 0 else part + one
    tmp[...] = part
    for at in range(2 * ny):
        mine = pl.multiple_of(at * 16 + c * 8, 8)
        other = pl.multiple_of(at * 16 + (1 - c) * 8, 8)
        keep_ref[at] = tmp[pl.ds(mine, 8), :]
        send_ref[at] = tmp[pl.ds(other, 8), :]


def window_kernel(
    meta, h, a_own, a_prev, a_after, x_far, l_far, p0, p1, p2, p3, own, prev, after, far_low, far_high,
    b0, b1, b2, b3, bulk_left, bulk_keep, bulk_send, left_0, left_1, left_2, left_3, keep_out, send_out,
    xs, ls, xb, ys, yb, raw, th, tmp, left, keep_rows, send_rows, sem, sem_y, sem_r, sem_b, sem_out,
):
    c, zh, first = meta[0], meta[1], meta[3]
    ny, block, width, cols = 4, 64, 1024, 512
    rows = [slice(n * block, (n + 1) * block) for n in range(ny)]
    early = [
        pltpu.make_async_copy(part, xs.at[rows[n], :], sem.at[n])
        for n, part in enumerate((a_own.at[0], a_prev.at[0], a_after.at[0], x_far))
    ]
    early += row_copies((p0, p1, p2, p3), 0, cols, ys.at[:, 0:cols], zh, c, sem_y)
    edge = row_copies((b0, b1, b2, b3), 0, cols, yb, zh, c, sem_b)
    proj = row_copies((p0, p1, p2, p3), cols, 2 * cols, ys.at[:, cols : 2 * cols], zh, c, sem_r)
    bulk = [
        pltpu.make_async_copy(part, xb.at[rows[n], :], sem.at[4 + n])
        for n, part in enumerate((own, prev, after))
    ]
    bulk.append(pltpu.make_async_copy(far_low, xb.at[rows[3], 0:width], sem.at[7]))
    bulk.append(pltpu.make_async_copy(far_high, xb.at[rows[3], width : 2 * width], sem.at[8]))
    late = [
        pltpu.make_async_copy(part, ls.at[rows[n], :], sem.at[9 + n])
        for n, part in enumerate((a_own.at[1], a_prev.at[1], a_after.at[1], l_far))
    ]
    late.append(pltpu.make_async_copy(bulk_keep, keep_rows.at[:, block : block + 8, :], sem.at[13]))
    late.append(pltpu.make_async_copy(bulk_send, send_rows.at[:, block : block + 8, :], sem.at[14]))
    for n in range(ny):
        proj.append(
            pltpu.make_async_copy(
                bulk_left.at[n], left.at[rows[n], 2 * width : 2 * width + 256], sem.at[15 + n]
            )
        )
    for copy in early:
        copy.start()

    @pl.when(first == 1)
    def _():
        for copy in edge:
            copy.start()

    for copy in proj:
        copy.start()

    @pl.when(first == 1)
    def _():
        for copy in bulk:
            copy.start()

    for copy in late:
        copy.start()
    for copy in early:
        copy.wait()

    @pl.when(first == 1)
    def _():
        for copy in edge:
            copy.wait()
        theta(h, 0, lambda s: xs[:, s * width : (s + 1) * width], yb[...], raw, th)

    @pl.when(first == 0)
    def _():
        theta(h, 0, lambda s: xs[:, s * width : (s + 1) * width], ys[:, 0:cols], raw, th)

    for copy in proj:
        copy.wait()

    def left_chunk(n, _):
        k_at = pl.multiple_of(n * 256, 256)
        r_part = ys[pl.ds(k_at, 256), cols : 2 * cols]
        for s in range(2):
            lanes = pl.ds(pl.multiple_of(s * width + n * 256, 256), 256)
            left[:, lanes] = dot(th[s], r_part, ((1,), (1,))).astype(BF16)
        return 0

    lax.fori_loop(0, 4, left_chunk, 0)
    outs = [
        pltpu.make_async_copy(left.at[rows[n], :], ref, sem_out.at[n])
        for n, ref in enumerate((left_0, left_1, left_2, left_3))
    ]
    for copy in outs:
        copy.start()

    @pl.when(first == 1)
    def _():
        for copy in bulk:
            copy.wait()
        theta(h, 16, lambda s: xb[:, s * width : (s + 1) * width], ys[:, 0:cols], raw, th)

    for copy in late:
        copy.wait()

    def right_chunk(n, _):
        part = None
        for s in range(2):
            l_part = ls[:, pl.ds(pl.multiple_of(s * width + n * 256, 256), 256)]
            one = dot(l_part, th[s], ((0,), (0,)))
            part = one if s == 0 else part + one
        tmp[...] = part
        for j in range(2):
            mine = pl.multiple_of(j * 128 + c * block, block)
            other = pl.multiple_of(j * 128 + (1 - c) * block, block)
            keep_rows[2 * n + j, 0:block, :] = tmp[pl.ds(mine, block), :]
            send_rows[2 * n + j, 0:block, :] = tmp[pl.ds(other, block), :]
        return 0

    lax.fori_loop(0, 4, right_chunk, 0)
    outs.append(pltpu.make_async_copy(send_rows, send_out, sem_out.at[4]))
    outs.append(pltpu.make_async_copy(keep_rows, keep_out, sem_out.at[5]))
    for copy in outs[4:]:
        copy.start()
    for copy in outs:
        copy.wait()


def call(kernel, outs, out_space, scratch, flops, meta, h, *arrays):
    smem = pl.BlockSpec(memory_space=pltpu.SMEM)
    anywhere = pl.BlockSpec(memory_space=pltpu.HBM)
    return pl.pallas_call(
        kernel,
        out_shape=outs,
        in_specs=[smem, smem] + [anywhere] * len(arrays),
        out_specs=(pl.BlockSpec(memory_space=out_space),) * len(outs),
        scratch_shapes=scratch,
        compiler_params=pltpu.CompilerParams(vmem_limit_bytes=VMEM_BYTES),
        cost_estimate=pl.CostEstimate(
            flops=flops, bytes_accessed=10_000_000, transcendentals=0
        ),
    )(meta, h, *arrays)


def ends_kernel(left, got, out):
    lows = [left[8 * k : 8 * (k + 1), :] for k in range(8)]
    rights = [got[q, 64:72].astype(F32) + got[4 + q, 64:72].astype(F32) for q in range(4)]
    rights = [rights[q][:, t * 256 : (t + 1) * 256] for t in range(2) for q in range(4)]
    ends = jnp.concatenate(
        [jnp.concatenate(lows, axis=1), jnp.concatenate(rights, axis=1)], axis=0
    ).astype(BF16)
    for g in range(8):
        out[g] = ends


def bulk_ends(left, got):
    return pl.pallas_call(
        ends_kernel,
        out_shape=jax.ShapeDtypeStruct((8, 16, 2048), BF16),
        cost_estimate=pl.CostEstimate(flops=1_000_000, bytes_accessed=700_000, transcendentals=0),
        name="finish",
    )(left, got)


def bulk_bond(meta, h, *arrays):
    sums = jax.ShapeDtypeStruct((8, 8, 512), F32)
    return call(
        bulk_kernel,
        (jax.ShapeDtypeStruct((4, 64, 256), BF16), sums, sums),
        pltpu.VMEM,
        [
            pltpu.VMEM((256, 2048), BF16),
            pltpu.VMEM((1024, 1024), BF16),
            pltpu.VMEM((4, 64, 256), BF16),
            pltpu.VMEM((2, 256, 512), F32),
            pltpu.VMEM((2, 256, 512), F32),
            pltpu.VMEM((128, 512), F32),
            pltpu.VMEM((4, 64, 256), F32),
            pltpu.SemaphoreType.DMA((6,)),
            pltpu.SemaphoreType.DMA((16,)),
        ],
        1_000_000_000,
        meta,
        h,
        *arrays,
    )


def window_bonds(meta, h, *arrays):
    rows = jax.ShapeDtypeStruct((64, 2304), BF16)
    sums = jax.ShapeDtypeStruct((8, 72, 512), F32)
    return call(
        window_kernel,
        (rows, rows, rows, rows, sums, sums),
        pltpu.HBM,
        [
            pltpu.VMEM((256, 2048), BF16),
            pltpu.VMEM((256, 2048), BF16),
            pltpu.VMEM((256, 2048), BF16),
            pltpu.VMEM((1024, 1024), BF16),
            pltpu.VMEM((1024, 512), BF16),
            pltpu.VMEM((2, 256, 512), F32),
            pltpu.VMEM((2, 256, 512), BF16),
            pltpu.VMEM((256, 512), F32),
            pltpu.VMEM((256, 2304), BF16),
            pltpu.VMEM((8, 72, 512), F32),
            pltpu.VMEM((8, 72, 512), F32),
            pltpu.SemaphoreType.DMA((19,)),
            pltpu.SemaphoreType.DMA((16,)),
            pltpu.SemaphoreType.DMA((16,)),
            pltpu.SemaphoreType.DMA((16,)),
            pltpu.SemaphoreType.DMA((6,)),
        ],
        3_000_000_000,
        meta,
        h,
        *arrays,
    )


def join_kernel(meta, got, returned, out):
    row = lax.broadcasted_iota(jnp.int32, (64, 1), 0) + meta[5] * 64
    keep = jnp.where(row < meta[6], 1.0, 0.0).astype(F32)
    for q in range(4):
        part = (got[q, 0:64].astype(F32) + got[4 + q, 0:64].astype(F32)) * keep
        for t in range(2):
            at = t * 1024 + q * 256
            out[0, :, at : at + 256] = part[:, t * 256 : (t + 1) * 256].astype(BF16)
    out[1] = returned[...]


def join(meta, got, returned):
    vmem = pl.BlockSpec(memory_space=pltpu.VMEM)
    return pl.pallas_call(
        join_kernel,
        out_shape=jax.ShapeDtypeStruct((2, 64, 2048), BF16),
        in_specs=[pl.BlockSpec(memory_space=pltpu.SMEM), vmem, vmem],
        out_specs=vmem,
        cost_estimate=pl.CostEstimate(flops=1_000_000, bytes_accessed=1_300_000, transcendentals=0),
        name="join",
    )(meta, got, returned)


def half_step(
    sites,
    proj_left,
    proj_right,
    edge_right,
    bulk_first,
    bulk_second,
    bulk_left_proj,
    bulk_right_proj,
    gate,
    gate_mask,
    bond_dims,
):
    block = sites.shape[1]
    width = sites.shape[2] // 2
    groups = lax.axis_size(SITE)
    ny = lax.axis_size("y")
    here = lax.axis_index(SITE)
    zh, y, c = (lax.axis_index(name) for name in BOND)
    first_group = here == 0
    identity = jnp.eye(4, dtype=F32)
    weight = gate_mask[0].astype(F32)
    mixer = weight * gate + (1.0 - weight) * identity
    mixer_left = jnp.where(first_group, gate, mixer)
    positions = jnp.arange(width, dtype=jnp.int32)
    keep = (positions < bond_dims[0]).astype(F32)
    keep_left = jnp.where(first_group, 1.0, keep)
    around = [(g, (g + 1) % groups) for g in range(groups)]

    meta = jnp.stack(
        [c, zh, y, first_group.astype(jnp.int32), here, lax.axis_index(BOND), bond_dims[0]]
    ).astype(jnp.int32)
    h = jnp.concatenate([mixer_left.reshape(16), mixer.reshape(16), gate.reshape(16)])
    up = [(k, (k + 1) % ny) for k in range(ny)]
    down = [(b, a) for a, b in up]
    back = [(b, a) for a, b in around]

    def exchange(v, axis):
        return lax.all_to_all(v, axis, split_axis=0, concat_axis=0, tiled=True)

    pair = [(0, 1), (1, 0)]

    x_own = lax.ppermute(sites[sites.shape[0] - 1], SITE, around)
    b_prev = lax.ppermute(bulk_second, "y", up)
    b_after = lax.ppermute(bulk_second, "y", down)

    quarters, bulk_quarters = split(
        meta, sites, edge_right, proj_right, bulk_first, bulk_right_proj, bulk_left_proj
    )
    q0 = exchange(bulk_quarters, "y")
    q1 = lax.ppermute(q0, "zh", pair)
    q2 = lax.ppermute(q0, "c", pair)
    q3 = lax.ppermute(q1, "c", pair)
    b_low = lax.ppermute(b_prev[:, :width], "y", up)
    b_high = lax.ppermute(b_after[:, width:], "y", down)
    p0 = exchange(quarters, "y")
    p1 = lax.ppermute(p0, "zh", pair)
    p2 = lax.ppermute(p0, "c", pair)
    p3 = lax.ppermute(p1, "c", pair)
    a_own = jnp.stack([x_own, proj_left[0]])
    a_prev = lax.ppermute(a_own, "y", up)
    a_after = lax.ppermute(a_own, "y", down)
    x_cut = a_prev[0]
    l_cut = a_after[1]
    x_far = lax.ppermute(x_cut, "y", up)
    l_far = lax.ppermute(l_cut, "y", down)

    bulk_rows = (bulk_second, b_prev, b_after, b_low, b_high)
    bulk_parts = bulk_bond(meta, h, *bulk_rows, q0, q1, q2, q3)
    left, left_down, left_up, left_far, right_own, right_send = window_bonds(
        meta, h, a_own, a_prev, a_after, x_far, l_far, p0, p1, p2, p3, *bulk_rows, q0, q1, q2, q3,
        *bulk_parts,
    )
    got = lax.ppermute(right_send, "c", pair)
    left_down = lax.ppermute(left_down, "y", down)
    left_up = lax.ppermute(left_up, "y", up)
    left_far = lax.ppermute(left_far, "y", [(k, (k + 2) % ny) for k in range(ny)])
    right = (right_own + got).astype(BF16)
    got = exchange(right, ("zh", "y"))
    left = sum(v.astype(F32) for v in (left, left_down, left_up, left_far))
    bulk_left = left[:, 2 * width :]
    left = left[:, : 2 * width] * jnp.concatenate([keep_left, keep_left])
    left = left.astype(BF16)
    returned = lax.ppermute(left, SITE, back)
    ends = bulk_ends(bulk_left, got)
    ends = exchange(ends, SITE)
    new_sites = join(meta, got, returned)
    new_second = ends[:, :8].reshape(block, 2 * width)
    new_first = ends[:, 8:].reshape(block, 2 * width)
    return new_sites, new_first, new_second


def solution(mesh):
    finer = Mesh(mesh.devices.reshape(4, 2, 2, 4, 2), SITE + BOND)
    rows = P(BOND, None)
    stacked = P(SITE, BOND, None)
    placed = (stacked,) * 3 + (rows,) * 5 + (P(), P(SITE), P(SITE))
    return jax.shard_map(
        half_step,
        mesh=finer,
        in_specs=placed,
        out_specs=(stacked, rows, rows),
        check_vma=False,
    )
```

```python
import jax
import jax.numpy as jnp
from jax import lax
from jax.experimental import pallas as pl
from jax.experimental.pallas import tpu as pltpu
from jax.sharding import Mesh
from jax.sharding import PartitionSpec as P


SITE = ("x", "zl")
BOND = ("zh", "y", "c")
VMEM_BYTES = 60 * 1024 * 1024
F32 = jnp.float32
BF16 = jnp.bfloat16


def dot(a, b, dims):
    return lax.dot_general(a, b, (dims, ((), ())), preferred_element_type=F32)


def split_kernel(meta, site, edge, proj, bulk, bulk_proj, bulk_left, out_ref, bulk_ref):
    first, g = meta[3], meta[4]
    quarter, width = 256, 1024
    column = lax.broadcasted_iota(jnp.int32, (width, 128), 1)
    source = (column // 8) * 64 + g * 8 + column % 8
    chosen = jnp.where(lax.broadcasted_iota(jnp.int32, (width, 128), 0) == source, 1.0, 0.0)
    chosen = chosen.astype(BF16)
    for s in range(2):
        part = dot(bulk_left[:, s * width : (s + 1) * width], chosen, ((1,), (0,))).astype(BF16)
        for q in range(4):
            bulk_ref[q, :, width + s * 128 : width + (s + 1) * 128] = part
    for q in range(4):
        for t in range(2):
            cols = slice(t * width + q * quarter, t * width + (q + 1) * quarter)
            low = slice(t * quarter, (t + 1) * quarter)
            high = slice((2 + t) * quarter, (3 + t) * quarter)
            out_ref[q, :, low] = site[0, :, cols]
            bulk_ref[q, :, low] = bulk[:, cols]
            out_ref[q, :, high] = jnp.where(first == 1, edge[:, cols], proj[0, :, cols])
            bulk_ref[q, :, high] = bulk_proj[:, cols]


def split(meta, sites, edge, proj, bulk, bulk_proj, bulk_left):
    smem = pl.BlockSpec(memory_space=pltpu.SMEM)
    one = pl.BlockSpec((1, 64, 2048), lambda i: (0, 0, 0))
    flat = pl.BlockSpec((64, 2048), lambda i: (0, 0))
    return pl.pallas_call(
        split_kernel,
        grid=(1,),
        out_shape=(
            jax.ShapeDtypeStruct((4, 64, 1024), BF16),
            jax.ShapeDtypeStruct((4, 64, 1280), BF16),
        ),
        in_specs=[smem, one, flat, one, flat, flat, flat],
        out_specs=(
            pl.BlockSpec((4, 64, 1024), lambda i: (0, 0, 0)),
            pl.BlockSpec((4, 64, 1280), lambda i: (0, 0, 0)),
        ),
        cost_estimate=pl.CostEstimate(
            flops=40_000_000, bytes_accessed=3_000_000, transcendentals=0
        ),
        name="split",
    )(meta, sites, edge, proj, bulk, bulk_proj, bulk_left)


def theta(h, base, x_of, y_part, raw, out):
    for s0 in range(2):
        raw[s0] = dot(x_of(s0), y_part, ((1,), (0,)))
    step, half = 32, 256

    def chunk(i, _):
        r = pl.ds(pl.multiple_of(i * step, step), step)
        parts = [raw[k // 2, r, (k % 2) * half : (k % 2 + 1) * half] for k in range(4)]
        for s in range(2):
            for t in range(2):
                row = base + 4 * (2 * s + t)
                val = h[row] * parts[0]
                for k in range(1, 4):
                    val = val + h[row + k] * parts[k]
                out[s, r, t * half : (t + 1) * half] = val.astype(out.dtype)
        return 0

    lax.fori_loop(0, 256 // step, chunk, 0, unroll=True)


def row_copies(parts, low, high, ys, zh, c, sem):
    copies = []
    for n, part in enumerate(parts):
        z_of = lax.rem(zh + n % 2, 2)
        c_of = lax.rem(c + n // 2, 2)
        for y in range(4):
            at = pl.multiple_of((z_of * 8 + y * 2 + c_of) * 64, 64)
            copies.append(
                pltpu.make_async_copy(
                    part.at[y, :, low:high], ys.at[pl.ds(at, 64), :], sem.at[n * 4 + y]
                )
            )
    return copies


def bulk_kernel(
    meta, h, own, prev, after, far_low, far_high, l_parts, b0, b1, b2, b3,
    left_ref, keep_ref, send_ref, xs, ys, rs, ls, raw, th, tmp, sem, sem_y,
):
    c, zh, me, g = meta[0], meta[1], meta[2], meta[4]
    ny, block, width, cols = 4, 64, 1024, 512
    owner = [lax.rem(me + d, ny) for d in (0, 3, 1, 2)]
    copies = row_copies((b0, b1, b2, b3), 0, cols, ys, zh, c, sem_y)
    for n, part in enumerate((b0, b1, b2, b3)):
        to = rs.at[n % 2, pl.ds(pl.multiple_of(lax.rem(c + n // 2, 2) * block, block), block), :]
        copies.append(pltpu.make_async_copy(part.at[ny], to, sem.at[6 + n]))
    for n, part in enumerate((own, prev, after)):
        copies.append(pltpu.make_async_copy(part, xs.at[n * block : (n + 1) * block, :], sem.at[n]))
    last = slice(3 * block, 4 * block)
    copies.append(pltpu.make_async_copy(far_low, xs.at[last, 0:width], sem.at[3]))
    copies.append(pltpu.make_async_copy(far_high, xs.at[last, width : 2 * width], sem.at[4]))
    copies.append(pltpu.make_async_copy(l_parts.at[:, :, width : width + 256], ls, sem.at[5]))
    for copy in copies:
        copy.start()
    for copy in copies:
        copy.wait()

    theta(h, 32, lambda s: xs[:, s * width : (s + 1) * width], ys[...], raw, th)
    far = lax.rem(lax.div(g, ny) + zh, 2)
    part = None
    for s in range(2):
        here = th[s].astype(BF16)
        left = dot(here, rs[far], ((1,), (1,))).astype(BF16)
        for j in range(ny):
            left_ref[j, :, s * 128 : (s + 1) * 128] = left[j * block : (j + 1) * block]
        for j in range(ny):
            l_part = ls[owner[j], :, s * 128 : (s + 1) * 128]
            one = dot(l_part, here[j * block : (j + 1) * block], ((0,), (0,)))
            part = one if part is None else part + one
    tmp[...] = part
    for at in range(2 * ny):
        mine = pl.multiple_of(at * 16 + c * 8, 8)
        other = pl.multiple_of(at * 16 + (1 - c) * 8, 8)
        keep_ref[at] = tmp[pl.ds(mine, 8), :]
        send_ref[at] = tmp[pl.ds(other, 8), :]


def window_kernel(
    meta, h, a_own, a_prev, a_after, x_far, l_far, p0, p1, p2, p3, own, prev, after, far_low, far_high,
    b0, b1, b2, b3, bulk_left, bulk_keep, bulk_send, left_0, left_1, left_2, left_3, keep_out, send_out,
    xs, ls, xb, ys, yb, raw, th, tmp, left, keep_rows, send_rows, sem, sem_y, sem_r, sem_b, sem_out,
):
    c, zh, first = meta[0], meta[1], meta[3]
    ny, block, width, cols = 4, 64, 1024, 512
    rows = [slice(n * block, (n + 1) * block) for n in range(ny)]
    early = [
        pltpu.make_async_copy(part, xs.at[rows[n], :], sem.at[n])
        for n, part in enumerate((a_own.at[0], a_prev.at[0], a_after.at[0], x_far))
    ]
    early += row_copies((p0, p1, p2, p3), 0, cols, ys.at[:, 0:cols], zh, c, sem_y)
    edge = row_copies((b0, b1, b2, b3), 0, cols, yb, zh, c, sem_b)
    proj = row_copies((p0, p1, p2, p3), cols, 2 * cols, ys.at[:, cols : 2 * cols], zh, c, sem_r)
    bulk = [
        pltpu.make_async_copy(part, xb.at[rows[n], :], sem.at[4 + n])
        for n, part in enumerate((own, prev, after))
    ]
    bulk.append(pltpu.make_async_copy(far_low, xb.at[rows[3], 0:width], sem.at[7]))
    bulk.append(pltpu.make_async_copy(far_high, xb.at[rows[3], width : 2 * width], sem.at[8]))
    late = [
        pltpu.make_async_copy(part, ls.at[rows[n], :], sem.at[9 + n])
        for n, part in enumerate((a_own.at[1], a_prev.at[1], a_after.at[1], l_far))
    ]
    late.append(pltpu.make_async_copy(bulk_keep, keep_rows.at[:, block : block + 8, :], sem.at[13]))
    late.append(pltpu.make_async_copy(bulk_send, send_rows.at[:, block : block + 8, :], sem.at[14]))
    for n in range(ny):
        proj.append(
            pltpu.make_async_copy(
                bulk_left.at[n], left.at[rows[n], 2 * width : 2 * width + 256], sem.at[15 + n]
            )
        )
    for copy in early:
        copy.start()

    @pl.when(first == 1)
    def _():
        for copy in edge:
            copy.start()

    for copy in proj:
        copy.start()

    @pl.when(first == 1)
    def _():
        for copy in bulk:
            copy.start()

    for copy in late:
        copy.start()
    for copy in early:
        copy.wait()

    @pl.when(first == 1)
    def _():
        for copy in edge:
            copy.wait()
        theta(h, 0, lambda s: xs[:, s * width : (s + 1) * width], yb[...], raw, th)

    @pl.when(first == 0)
    def _():
        theta(h, 0, lambda s: xs[:, s * width : (s + 1) * width], ys[:, 0:cols], raw, th)

    for copy in proj:
        copy.wait()

    def left_chunk(n, _):
        k_at = pl.multiple_of(n * 256, 256)
        r_part = ys[pl.ds(k_at, 256), cols : 2 * cols]
        for s in range(2):
            lanes = pl.ds(pl.multiple_of(s * width + n * 256, 256), 256)
            left[:, lanes] = dot(th[s], r_part, ((1,), (1,))).astype(BF16)
        return 0

    lax.fori_loop(0, 4, left_chunk, 0, unroll=True)
    outs = [
        pltpu.make_async_copy(left.at[rows[n], :], ref, sem_out.at[n])
        for n, ref in enumerate((left_0, left_1, left_2, left_3))
    ]
    for copy in outs:
        copy.start()

    @pl.when(first == 1)
    def _():
        for copy in bulk:
            copy.wait()
        theta(h, 16, lambda s: xb[:, s * width : (s + 1) * width], ys[:, 0:cols], raw, th)

    for copy in late:
        copy.wait()

    def right_chunk(n, _):
        part = None
        for s in range(2):
            l_part = ls[:, pl.ds(pl.multiple_of(s * width + n * 256, 256), 256)]
            one = dot(l_part, th[s], ((0,), (0,)))
            part = one if s == 0 else part + one
        tmp[...] = part
        for j in range(2):
            mine = pl.multiple_of(j * 128 + c * block, block)
            other = pl.multiple_of(j * 128 + (1 - c) * block, block)
            keep_rows[2 * n + j, 0:block, :] = tmp[pl.ds(mine, block), :]
            send_rows[2 * n + j, 0:block, :] = tmp[pl.ds(other, block), :]
        return 0

    lax.fori_loop(0, 4, right_chunk, 0, unroll=True)
    outs.append(pltpu.make_async_copy(send_rows, send_out, sem_out.at[4]))
    outs.append(pltpu.make_async_copy(keep_rows, keep_out, sem_out.at[5]))
    for copy in outs[4:]:
        copy.start()
    for copy in outs:
        copy.wait()


def call(kernel, outs, out_space, scratch, flops, meta, h, *arrays):
    smem = pl.BlockSpec(memory_space=pltpu.SMEM)
    anywhere = pl.BlockSpec(memory_space=pltpu.HBM)
    return pl.pallas_call(
        kernel,
        out_shape=outs,
        in_specs=[smem, smem] + [anywhere] * len(arrays),
        out_specs=(pl.BlockSpec(memory_space=out_space),) * len(outs),
        scratch_shapes=scratch,
        compiler_params=pltpu.CompilerParams(vmem_limit_bytes=VMEM_BYTES),
        cost_estimate=pl.CostEstimate(
            flops=flops, bytes_accessed=10_000_000, transcendentals=0
        ),
    )(meta, h, *arrays)


def ends_kernel(left, got, out):
    rights = [got[q].astype(F32) + got[4 + q].astype(F32) for q in range(4)]
    rights = [rights[q][:, t * 256 : (t + 1) * 256] for t in range(2) for q in range(4)]
    rights = jnp.concatenate(rights, axis=0).astype(BF16)
    lefts = left[...].astype(BF16)
    for g in range(8):
        out[g, :, 0:256] = lefts
        out[g, :, 256:512] = rights


def bulk_ends(left, got):
    return pl.pallas_call(
        ends_kernel,
        grid=(1,),
        in_specs=[
            pl.BlockSpec((64, 256), lambda i: (0, 0)),
            pl.BlockSpec((8, 8, 512), lambda i: (0, 8, 0)),
        ],
        out_specs=pl.BlockSpec((8, 64, 512), lambda i: (0, 0, 0)),
        out_shape=jax.ShapeDtypeStruct((8, 64, 512), BF16),
        cost_estimate=pl.CostEstimate(flops=1_000_000, bytes_accessed=700_000, transcendentals=0),
        name="finish",
    )(left, got)


def spread_kernel(ends, first, second):
    for g in range(8):
        for s in range(2):
            second[:, s * 1024 + g * 128 : s * 1024 + (g + 1) * 128] = ends[
                g, :, s * 128 : (s + 1) * 128
            ]
    for pair in range(4):
        rows = []
        for g in (2 * pair, 2 * pair + 1):
            right = ends[g, :, 256:512].astype(F32)
            rows.append(jnp.concatenate([right[8 * k : 8 * (k + 1)] for k in range(8)], axis=1))
        first[16 * pair : 16 * (pair + 1), :] = jnp.concatenate(rows, axis=0).astype(BF16)


def spread(ends):
    rows = jax.ShapeDtypeStruct((64, 2048), BF16)
    return pl.pallas_call(
        spread_kernel,
        out_shape=(rows, rows),
        cost_estimate=pl.CostEstimate(flops=1_000_000, bytes_accessed=1_000_000, transcendentals=0),
        name="spread",
    )(ends)


def bulk_bond(meta, h, *arrays):
    sums = jax.ShapeDtypeStruct((8, 8, 512), F32)
    return call(
        bulk_kernel,
        (jax.ShapeDtypeStruct((4, 64, 256), BF16), sums, sums),
        pltpu.VMEM,
        [
            pltpu.VMEM((256, 2048), BF16),
            pltpu.VMEM((1024, 512), BF16),
            pltpu.VMEM((2, 128, 512), BF16),
            pltpu.VMEM((4, 64, 256), BF16),
            pltpu.VMEM((2, 256, 512), F32),
            pltpu.VMEM((2, 256, 512), F32),
            pltpu.VMEM((128, 512), F32),
            pltpu.SemaphoreType.DMA((10,)),
            pltpu.SemaphoreType.DMA((16,)),
        ],
        1_000_000_000,
        meta,
        h,
        *arrays,
    )


def window_bonds(meta, h, *arrays):
    rows = jax.ShapeDtypeStruct((64, 2304), BF16)
    sums = jax.ShapeDtypeStruct((8, 72, 512), F32)
    return call(
        window_kernel,
        (rows, rows, rows, rows, sums, sums),
        pltpu.HBM,
        [
            pltpu.VMEM((256, 2048), BF16),
            pltpu.VMEM((256, 2048), BF16),
            pltpu.VMEM((256, 2048), BF16),
            pltpu.VMEM((1024, 1024), BF16),
            pltpu.VMEM((1024, 512), BF16),
            pltpu.VMEM((2, 256, 512), F32),
            pltpu.VMEM((2, 256, 512), BF16),
            pltpu.VMEM((256, 512), F32),
            pltpu.VMEM((256, 2304), BF16),
            pltpu.VMEM((8, 72, 512), F32),
            pltpu.VMEM((8, 72, 512), F32),
            pltpu.SemaphoreType.DMA((19,)),
            pltpu.SemaphoreType.DMA((16,)),
            pltpu.SemaphoreType.DMA((16,)),
            pltpu.SemaphoreType.DMA((16,)),
            pltpu.SemaphoreType.DMA((6,)),
        ],
        3_000_000_000,
        meta,
        h,
        *arrays,
    )


def join_kernel(meta, got, returned, out):
    row = lax.broadcasted_iota(jnp.int32, (64, 1), 0) + meta[5] * 64
    keep = jnp.where(row < meta[6], 1.0, 0.0).astype(F32)
    for q in range(4):
        part = (got[q, 0:64].astype(F32) + got[4 + q, 0:64].astype(F32)) * keep
        for t in range(2):
            at = t * 1024 + q * 256
            out[0, :, at : at + 256] = part[:, t * 256 : (t + 1) * 256].astype(BF16)
    out[1] = returned[...]


def join(meta, got, returned):
    vmem = pl.BlockSpec(memory_space=pltpu.VMEM)
    return pl.pallas_call(
        join_kernel,
        out_shape=jax.ShapeDtypeStruct((2, 64, 2048), BF16),
        in_specs=[pl.BlockSpec(memory_space=pltpu.SMEM), vmem, vmem],
        out_specs=vmem,
        cost_estimate=pl.CostEstimate(flops=1_000_000, bytes_accessed=1_300_000, transcendentals=0),
        name="join",
    )(meta, got, returned)


def half_step(
    sites,
    proj_left,
    proj_right,
    edge_right,
    bulk_first,
    bulk_second,
    bulk_left_proj,
    bulk_right_proj,
    gate,
    gate_mask,
    bond_dims,
):
    width = sites.shape[2] // 2
    groups = lax.axis_size(SITE)
    ny = lax.axis_size("y")
    here = lax.axis_index(SITE)
    zh, y, c = (lax.axis_index(name) for name in BOND)
    first_group = here == 0
    identity = jnp.eye(4, dtype=F32)
    weight = gate_mask[0].astype(F32)
    mixer = weight * gate + (1.0 - weight) * identity
    mixer_left = jnp.where(first_group, gate, mixer)
    positions = jnp.arange(width, dtype=jnp.int32)
    keep = (positions < bond_dims[0]).astype(F32)
    keep_left = jnp.where(first_group, 1.0, keep)
    around = [(g, (g + 1) % groups) for g in range(groups)]

    meta = jnp.stack(
        [c, zh, y, first_group.astype(jnp.int32), here, lax.axis_index(BOND), bond_dims[0]]
    ).astype(jnp.int32)
    h = jnp.concatenate([mixer_left.reshape(16), mixer.reshape(16), gate.reshape(16)])
    up = [(k, (k + 1) % ny) for k in range(ny)]
    down = [(b, a) for a, b in up]
    back = [(b, a) for a, b in around]

    def exchange(v, axis):
        return lax.all_to_all(v, axis, split_axis=0, concat_axis=0, tiled=True)

    pair = [(0, 1), (1, 0)]

    x_own = lax.ppermute(sites[sites.shape[0] - 1], SITE, around)
    b_prev = lax.ppermute(bulk_second, "y", up)
    b_after = lax.ppermute(bulk_second, "y", down)

    quarters, bulk_quarters = split(
        meta, sites, edge_right, proj_right, bulk_first, bulk_right_proj, bulk_left_proj
    )
    q0 = exchange(bulk_quarters, "y")
    chosen = lax.dynamic_index_in_dim(q0, lax.rem(here, ny), 0)[:, :, width // 2 : width]
    b_own = jnp.concatenate([q0[:, :, : width // 2], chosen], axis=0)
    q1 = lax.ppermute(b_own, "zh", pair)
    q2 = lax.ppermute(b_own, "c", pair)
    q3 = lax.ppermute(q1, "c", pair)
    b_low = b_prev[:, :width]
    b_high = b_after[:, width:]
    b_low = lax.ppermute(b_low, "y", up)
    b_high = lax.ppermute(b_high, "y", down)
    p0 = exchange(quarters, "y")
    p1 = lax.ppermute(p0, "zh", pair)
    p2 = lax.ppermute(p0, "c", pair)
    p3 = lax.ppermute(p1, "c", pair)
    a_own = jnp.stack([x_own, proj_left[0]])
    a_prev = lax.ppermute(a_own, "y", up)
    a_after = lax.ppermute(a_own, "y", down)
    x_cut = a_prev[0]
    l_cut = a_after[1]
    x_far = lax.ppermute(x_cut, "y", up)
    l_far = lax.ppermute(l_cut, "y", down)

    bulk_rows = (bulk_second, b_prev, b_after, b_low, b_high)
    bulk_parts = bulk_bond(meta, h, *bulk_rows, q0, b_own, q1, q2, q3)
    left, left_down, left_up, left_far, right_own, right_send = window_bonds(
        meta, h, a_own, a_prev, a_after, x_far, l_far, p0, p1, p2, p3, *bulk_rows, b_own, q1, q2, q3,
        *bulk_parts,
    )
    got = lax.ppermute(right_send, "c", pair)
    left_down = lax.ppermute(left_down, "y", down)
    left_up = lax.ppermute(left_up, "y", up)
    left_far = lax.ppermute(left_far, "y", [(k, (k + 2) % ny) for k in range(ny)])
    right = (right_own + got).astype(BF16)
    got = exchange(right, ("zh", "y"))
    left = sum(v.astype(F32) for v in (left, left_down, left_up, left_far))
    bulk_left = left[:, 2 * width :]
    left = left[:, : 2 * width] * jnp.concatenate([keep_left, keep_left])
    left = left.astype(BF16)
    returned = lax.ppermute(left, SITE, back)
    ends = bulk_ends(bulk_left, got)
    ends = exchange(ends, SITE)
    new_sites = join(meta, got, returned)
    new_first, new_second = spread(ends)
    return new_sites, new_first, new_second


def solution(mesh):
    finer = Mesh(mesh.devices.reshape(4, 2, 2, 4, 2), SITE + BOND)
    rows = P(BOND, None)
    stacked = P(SITE, BOND, None)
    placed = (stacked,) * 3 + (rows,) * 5 + (P(), P(SITE), P(SITE))
    return jax.shard_map(
        half_step,
        mesh=finer,
        in_specs=placed,
        out_specs=(stacked, rows, rows),
        check_vma=False,
    )
```

```python
import jax
import jax.numpy as jnp
from jax import lax
from jax.experimental import pallas as pl
from jax.experimental.pallas import tpu as pltpu
from jax.sharding import Mesh
from jax.sharding import PartitionSpec as P


SITE = ("x", "zl")
BOND = ("zh", "y", "c")
VMEM_BYTES = 60 * 1024 * 1024
F32 = jnp.float32
BF16 = jnp.bfloat16


def dot(a, b, dims):
    return lax.dot_general(a, b, (dims, ((), ())), preferred_element_type=F32)


def split_kernel(
    meta, site, edge, proj, bulk, bulk_proj, bulk_left, w_0, w_1, w_2, w_3, b_0, b_1, b_2, b_3
):
    me, first, g = meta[2], meta[3], meta[4]
    quarter, width = 256, 1024
    column = lax.broadcasted_iota(jnp.int32, (width, 128), 1)
    source = (column // 8) * 64 + g * 8 + column % 8
    chosen = jnp.where(lax.broadcasted_iota(jnp.int32, (width, 128), 0) == source, 1.0, 0.0)
    chosen = chosen.astype(BF16)
    for s in range(2):
        part = dot(bulk_left[:, s * width : (s + 1) * width], chosen, ((1,), (0,))).astype(BF16)
        for ref in (b_0, b_1, b_2, b_3):
            ref[:, width + s * 128 : width + (s + 1) * 128] = part
    for step, w_ref, b_ref in ((0, w_0, b_0), (1, w_1, b_1), (3, w_2, b_2), (2, w_3, b_3)):
        q = lax.rem(me + step, 4)
        for t in range(2):
            cols = pl.ds(pl.multiple_of(t * width + q * quarter, quarter), quarter)
            low = slice(t * quarter, (t + 1) * quarter)
            high = slice((2 + t) * quarter, (3 + t) * quarter)
            w_ref[:, low] = site[0, :, cols]
            b_ref[:, low] = bulk[:, cols]
            w_ref[:, high] = jnp.where(first == 1, edge[:, cols], proj[0, :, cols])
            b_ref[:, high] = bulk_proj[:, cols]


def split(meta, sites, edge, proj, bulk, bulk_proj, bulk_left):
    smem = pl.BlockSpec(memory_space=pltpu.SMEM)
    one = pl.BlockSpec((1, 64, 2048), lambda i: (0, 0, 0))
    flat = pl.BlockSpec((64, 2048), lambda i: (0, 0))
    return pl.pallas_call(
        split_kernel,
        grid=(1,),
        out_shape=(jax.ShapeDtypeStruct((64, 1024), BF16),) * 4
        + (jax.ShapeDtypeStruct((64, 1280), BF16),) * 4,
        in_specs=[smem, one, flat, one, flat, flat, flat],
        out_specs=(pl.BlockSpec((64, 1024), lambda i: (0, 0)),) * 4
        + (pl.BlockSpec((64, 1280), lambda i: (0, 0)),) * 4,
        cost_estimate=pl.CostEstimate(
            flops=40_000_000, bytes_accessed=3_000_000, transcendentals=0
        ),
        name="split",
    )(meta, sites, edge, proj, bulk, bulk_proj, bulk_left)


def theta(h, base, x_of, y_part, raw, out):
    for s0 in range(2):
        raw[s0] = dot(x_of(s0), y_part, ((1,), (0,)))
    step, half = 32, 256

    def chunk(i, _):
        r = pl.ds(pl.multiple_of(i * step, step), step)
        parts = [raw[k // 2, r, (k % 2) * half : (k % 2 + 1) * half] for k in range(4)]
        for s in range(2):
            for t in range(2):
                row = base + 4 * (2 * s + t)
                val = h[row] * parts[0]
                for k in range(1, 4):
                    val = val + h[row + k] * parts[k]
                out[s, r, t * half : (t + 1) * half] = val.astype(out.dtype)
        return 0

    lax.fori_loop(0, 256 // step, chunk, 0, unroll=True)


def row_copies(parts, low, high, ys, zh, c, me, sem):
    copies = []
    for n, part in enumerate(parts):
        z_of = lax.rem(zh + n % 2, 2)
        c_of = lax.rem(c + n // 2, 2)
        for y, step in enumerate((0, 3, 1, 2)):
            at = pl.multiple_of((z_of * 8 + lax.rem(me + step, 4) * 2 + c_of) * 64, 64)
            copies.append(
                pltpu.make_async_copy(
                    part.at[y, :, low:high], ys.at[pl.ds(at, 64), :], sem.at[n * 4 + y]
                )
            )
    return copies


def bulk_kernel(
    meta, h, own, prev, after, far_low, far_high, l_parts, b0, b1, b2, b3,
    left_ref, keep_ref, send_ref, xs, ys, rs, ls, raw, th, tmp, sem, sem_y,
):
    c, zh, me, g = meta[0], meta[1], meta[2], meta[4]
    ny, block, width, cols = 4, 64, 1024, 512
    copies = row_copies((b0, b1, b2, b3), 0, cols, ys, zh, c, me, sem_y)
    for n, part in enumerate((b0, b1, b2, b3)):
        to = rs.at[n % 2, pl.ds(pl.multiple_of(lax.rem(c + n // 2, 2) * block, block), block), :]
        copies.append(pltpu.make_async_copy(part.at[ny], to, sem.at[6 + n]))
    for n, part in enumerate((own, prev, after)):
        copies.append(pltpu.make_async_copy(part, xs.at[n * block : (n + 1) * block, :], sem.at[n]))
    last = slice(3 * block, 4 * block)
    copies.append(pltpu.make_async_copy(far_low, xs.at[last, 0:width], sem.at[3]))
    copies.append(pltpu.make_async_copy(far_high, xs.at[last, width : 2 * width], sem.at[4]))
    copies.append(pltpu.make_async_copy(l_parts.at[:, :, width : width + 256], ls, sem.at[5]))
    for copy in copies:
        copy.start()
    for copy in copies:
        copy.wait()

    theta(h, 32, lambda s: xs[:, s * width : (s + 1) * width], ys[...], raw, th)
    far = lax.rem(lax.div(g, ny) + zh, 2)
    part = None
    for s in range(2):
        here = th[s].astype(BF16)
        left = dot(here, rs[far], ((1,), (1,))).astype(BF16)
        for j in range(ny):
            left_ref[j, :, s * 128 : (s + 1) * 128] = left[j * block : (j + 1) * block]
        for j in range(ny):
            l_part = ls[j, :, s * 128 : (s + 1) * 128]
            one = dot(l_part, here[j * block : (j + 1) * block], ((0,), (0,)))
            part = one if part is None else part + one
    tmp[...] = part
    for at in range(2 * ny):
        mine = pl.multiple_of(at * 16 + c * 8, 8)
        other = pl.multiple_of(at * 16 + (1 - c) * 8, 8)
        keep_ref[at] = tmp[pl.ds(mine, 8), :]
        send_ref[at] = tmp[pl.ds(other, 8), :]


def window_kernel(
    meta, h, a_own, a_prev, a_after, x_far, l_far, p0, p1, p2, p3, own, prev, after, far_low, far_high,
    b0, b1, b2, b3, bulk_left, bulk_keep, bulk_send, left_0, left_1, left_2, left_3, keep_out, send_out,
    xs, ls, xb, ys, yb, raw, th, tmp, left, keep_rows, send_rows, sem, sem_y, sem_r, sem_b, sem_out,
):
    c, zh, me, first = meta[0], meta[1], meta[2], meta[3]
    ny, block, width, cols = 4, 64, 1024, 512
    rows = [slice(n * block, (n + 1) * block) for n in range(ny)]
    early = [
        pltpu.make_async_copy(part, xs.at[rows[n], :], sem.at[n])
        for n, part in enumerate((a_own.at[0], a_prev.at[0], a_after.at[0], x_far))
    ]
    early += row_copies((p0, p1, p2, p3), 0, cols, ys.at[:, 0:cols], zh, c, me, sem_y)
    edge = row_copies((b0, b1, b2, b3), 0, cols, yb, zh, c, me, sem_b)
    proj = row_copies((p0, p1, p2, p3), cols, 2 * cols, ys.at[:, cols : 2 * cols], zh, c, me, sem_r)
    bulk = [
        pltpu.make_async_copy(part, xb.at[rows[n], :], sem.at[4 + n])
        for n, part in enumerate((own, prev, after))
    ]
    bulk.append(pltpu.make_async_copy(far_low, xb.at[rows[3], 0:width], sem.at[7]))
    bulk.append(pltpu.make_async_copy(far_high, xb.at[rows[3], width : 2 * width], sem.at[8]))
    late = [
        pltpu.make_async_copy(part, ls.at[rows[n], :], sem.at[9 + n])
        for n, part in enumerate((a_own.at[1], a_prev.at[1], a_after.at[1], l_far))
    ]
    late.append(pltpu.make_async_copy(bulk_keep, keep_rows.at[:, block : block + 8, :], sem.at[13]))
    late.append(pltpu.make_async_copy(bulk_send, send_rows.at[:, block : block + 8, :], sem.at[14]))
    for n in range(ny):
        proj.append(
            pltpu.make_async_copy(
                bulk_left.at[n], left.at[rows[n], 2 * width : 2 * width + 256], sem.at[15 + n]
            )
        )
    for copy in early:
        copy.start()

    @pl.when(first == 1)
    def _():
        for copy in edge:
            copy.start()

    for copy in proj:
        copy.start()

    @pl.when(first == 1)
    def _():
        for copy in bulk:
            copy.start()

    for copy in late:
        copy.start()
    for copy in early:
        copy.wait()

    @pl.when(first == 1)
    def _():
        for copy in edge:
            copy.wait()
        theta(h, 0, lambda s: xs[:, s * width : (s + 1) * width], yb[...], raw, th)

    @pl.when(first == 0)
    def _():
        theta(h, 0, lambda s: xs[:, s * width : (s + 1) * width], ys[:, 0:cols], raw, th)

    for copy in proj:
        copy.wait()

    def left_chunk(n, _):
        k_at = pl.multiple_of(n * 256, 256)
        r_part = ys[pl.ds(k_at, 256), cols : 2 * cols]
        for s in range(2):
            lanes = pl.ds(pl.multiple_of(s * width + n * 256, 256), 256)
            left[:, lanes] = dot(th[s], r_part, ((1,), (1,))).astype(BF16)
        return 0

    lax.fori_loop(0, 4, left_chunk, 0, unroll=True)
    outs = [
        pltpu.make_async_copy(left.at[rows[n], :], ref, sem_out.at[n])
        for n, ref in enumerate((left_0, left_1, left_2, left_3))
    ]
    for copy in outs:
        copy.start()

    @pl.when(first == 1)
    def _():
        for copy in bulk:
            copy.wait()
        theta(h, 16, lambda s: xb[:, s * width : (s + 1) * width], ys[:, 0:cols], raw, th)

    for copy in late:
        copy.wait()

    def right_chunk(n, _):
        part = None
        for s in range(2):
            l_part = ls[:, pl.ds(pl.multiple_of(s * width + n * 256, 256), 256)]
            one = dot(l_part, th[s], ((0,), (0,)))
            part = one if s == 0 else part + one
        tmp[...] = part
        for j in range(2):
            mine = pl.multiple_of(j * 128 + c * block, block)
            other = pl.multiple_of(j * 128 + (1 - c) * block, block)
            keep_rows[2 * n + j, 0:block, :] = tmp[pl.ds(mine, block), :]
            send_rows[2 * n + j, 0:block, :] = tmp[pl.ds(other, block), :]
        return 0

    lax.fori_loop(0, 4, right_chunk, 0, unroll=True)
    outs.append(pltpu.make_async_copy(send_rows, send_out, sem_out.at[4]))
    outs.append(pltpu.make_async_copy(keep_rows, keep_out, sem_out.at[5]))
    for copy in outs[4:]:
        copy.start()
    for copy in outs:
        copy.wait()


def call(kernel, outs, out_space, scratch, flops, meta, h, *arrays):
    smem = pl.BlockSpec(memory_space=pltpu.SMEM)
    anywhere = pl.BlockSpec(memory_space=pltpu.HBM)
    return pl.pallas_call(
        kernel,
        out_shape=outs,
        in_specs=[smem, smem] + [anywhere] * len(arrays),
        out_specs=(pl.BlockSpec(memory_space=out_space),) * len(outs),
        scratch_shapes=scratch,
        compiler_params=pltpu.CompilerParams(vmem_limit_bytes=VMEM_BYTES),
        cost_estimate=pl.CostEstimate(
            flops=flops, bytes_accessed=10_000_000, transcendentals=0
        ),
    )(meta, h, *arrays)


def ends_kernel(left, got, out):
    rights = [got[q].astype(F32) + got[4 + q].astype(F32) for q in range(4)]
    rights = [rights[q][:, t * 256 : (t + 1) * 256] for t in range(2) for q in range(4)]
    rights = jnp.concatenate(rights, axis=0).astype(BF16)
    lefts = left[...].astype(BF16)
    for g in range(8):
        out[g, :, 0:256] = lefts
        out[g, :, 256:512] = rights


def bulk_ends(left, got):
    return pl.pallas_call(
        ends_kernel,
        grid=(1,),
        in_specs=[
            pl.BlockSpec((64, 256), lambda i: (0, 0)),
            pl.BlockSpec((8, 8, 512), lambda i: (0, 8, 0)),
        ],
        out_specs=pl.BlockSpec((8, 64, 512), lambda i: (0, 0, 0)),
        out_shape=jax.ShapeDtypeStruct((8, 64, 512), BF16),
        cost_estimate=pl.CostEstimate(flops=1_000_000, bytes_accessed=700_000, transcendentals=0),
        name="finish",
    )(left, got)


def spread_kernel(ends, first, second):
    for g in range(8):
        for s in range(2):
            second[:, s * 1024 + g * 128 : s * 1024 + (g + 1) * 128] = ends[
                g, :, s * 128 : (s + 1) * 128
            ]
    for pair in range(4):
        rows = []
        for g in (2 * pair, 2 * pair + 1):
            right = ends[g, :, 256:512].astype(F32)
            rows.append(jnp.concatenate([right[8 * k : 8 * (k + 1)] for k in range(8)], axis=1))
        first[16 * pair : 16 * (pair + 1), :] = jnp.concatenate(rows, axis=0).astype(BF16)


def spread(ends):
    rows = jax.ShapeDtypeStruct((64, 2048), BF16)
    return pl.pallas_call(
        spread_kernel,
        out_shape=(rows, rows),
        cost_estimate=pl.CostEstimate(flops=1_000_000, bytes_accessed=1_000_000, transcendentals=0),
        name="spread",
    )(ends)


def bulk_bond(meta, h, *arrays):
    sums = jax.ShapeDtypeStruct((8, 8, 512), F32)
    return call(
        bulk_kernel,
        (jax.ShapeDtypeStruct((4, 64, 256), BF16), sums, sums),
        pltpu.VMEM,
        [
            pltpu.VMEM((256, 2048), BF16),
            pltpu.VMEM((1024, 512), BF16),
            pltpu.VMEM((2, 128, 512), BF16),
            pltpu.VMEM((4, 64, 256), BF16),
            pltpu.VMEM((2, 256, 512), F32),
            pltpu.VMEM((2, 256, 512), F32),
            pltpu.VMEM((128, 512), F32),
            pltpu.SemaphoreType.DMA((10,)),
            pltpu.SemaphoreType.DMA((16,)),
        ],
        1_000_000_000,
        meta,
        h,
        *arrays,
    )


def window_bonds(meta, h, *arrays):
    rows = jax.ShapeDtypeStruct((64, 2304), BF16)
    sums = jax.ShapeDtypeStruct((8, 72, 512), F32)
    return call(
        window_kernel,
        (rows, rows, rows, rows, sums, sums),
        pltpu.HBM,
        [
            pltpu.VMEM((256, 2048), BF16),
            pltpu.VMEM((256, 2048), BF16),
            pltpu.VMEM((256, 2048), BF16),
            pltpu.VMEM((1024, 1024), BF16),
            pltpu.VMEM((1024, 512), BF16),
            pltpu.VMEM((2, 256, 512), F32),
            pltpu.VMEM((2, 256, 512), BF16),
            pltpu.VMEM((256, 512), F32),
            pltpu.VMEM((256, 2304), BF16),
            pltpu.VMEM((8, 72, 512), F32),
            pltpu.VMEM((8, 72, 512), F32),
            pltpu.SemaphoreType.DMA((19,)),
            pltpu.SemaphoreType.DMA((16,)),
            pltpu.SemaphoreType.DMA((16,)),
            pltpu.SemaphoreType.DMA((16,)),
            pltpu.SemaphoreType.DMA((6,)),
        ],
        3_000_000_000,
        meta,
        h,
        *arrays,
    )


def join_kernel(meta, got, returned, out):
    row = lax.broadcasted_iota(jnp.int32, (64, 1), 0) + meta[5] * 64
    keep = jnp.where(row < meta[6], 1.0, 0.0).astype(F32)
    for q in range(4):
        part = (got[q, 0:64].astype(F32) + got[4 + q, 0:64].astype(F32)) * keep
        for t in range(2):
            at = t * 1024 + q * 256
            out[0, :, at : at + 256] = part[:, t * 256 : (t + 1) * 256].astype(BF16)
    out[1] = returned[...]


def join(meta, got, returned):
    vmem = pl.BlockSpec(memory_space=pltpu.VMEM)
    return pl.pallas_call(
        join_kernel,
        out_shape=jax.ShapeDtypeStruct((2, 64, 2048), BF16),
        in_specs=[pl.BlockSpec(memory_space=pltpu.SMEM), vmem, vmem],
        out_specs=vmem,
        cost_estimate=pl.CostEstimate(flops=1_000_000, bytes_accessed=1_300_000, transcendentals=0),
        name="join",
    )(meta, got, returned)


def half_step(
    sites,
    proj_left,
    proj_right,
    edge_right,
    bulk_first,
    bulk_second,
    bulk_left_proj,
    bulk_right_proj,
    gate,
    gate_mask,
    bond_dims,
):
    width = sites.shape[2] // 2
    groups = lax.axis_size(SITE)
    ny = lax.axis_size("y")
    here = lax.axis_index(SITE)
    zh, y, c = (lax.axis_index(name) for name in BOND)
    first_group = here == 0
    identity = jnp.eye(4, dtype=F32)
    weight = gate_mask[0].astype(F32)
    mixer = weight * gate + (1.0 - weight) * identity
    mixer_left = jnp.where(first_group, gate, mixer)
    positions = jnp.arange(width, dtype=jnp.int32)
    keep = (positions < bond_dims[0]).astype(F32)
    keep_left = jnp.where(first_group, 1.0, keep)
    around = [(g, (g + 1) % groups) for g in range(groups)]

    meta = jnp.stack(
        [c, zh, y, first_group.astype(jnp.int32), here, lax.axis_index(BOND), bond_dims[0]]
    ).astype(jnp.int32)
    h = jnp.concatenate([mixer_left.reshape(16), mixer.reshape(16), gate.reshape(16)])
    up = [(k, (k + 1) % ny) for k in range(ny)]
    down = [(b, a) for a, b in up]
    back = [(b, a) for a, b in around]

    def exchange(v, axis):
        return lax.all_to_all(v, axis, split_axis=0, concat_axis=0, tiled=True)

    pair = [(0, 1), (1, 0)]

    x_own = lax.ppermute(sites[sites.shape[0] - 1], SITE, around)
    b_prev = lax.ppermute(bulk_second, "y", up)
    b_after = lax.ppermute(bulk_second, "y", down)

    across = [(k, (k + 2) % ny) for k in range(ny)]
    w_0, w_1, w_2, w_3, b_0, b_1, b_2, b_3 = split(
        meta, sites, edge_right, proj_right, bulk_first, bulk_right_proj, bulk_left_proj
    )
    b_1 = lax.ppermute(b_1, "y", up)
    b_2 = lax.ppermute(b_2, "y", down)
    b_3 = lax.ppermute(b_3, "y", across)
    w_1 = lax.ppermute(w_1, "y", up)
    w_2 = lax.ppermute(w_2, "y", down)
    w_3 = lax.ppermute(w_3, "y", across)
    q0 = jnp.stack([b_0, b_1, b_2, b_3])
    step = lax.rem(here + 2 * ny - y, ny)
    place = jnp.where(step == 0, 0, jnp.where(step == 3, 1, step + 1))
    chosen = lax.dynamic_index_in_dim(q0, place, 0)[:, :, width // 2 : width]
    b_own = jnp.concatenate([q0[:, :, : width // 2], chosen], axis=0)
    q1 = lax.ppermute(b_own, "zh", pair)
    q2 = lax.ppermute(b_own, "c", pair)
    q3 = lax.ppermute(q1, "c", pair)
    b_low = b_prev[:, :width]
    b_high = b_after[:, width:]
    b_low = lax.ppermute(b_low, "y", up)
    b_high = lax.ppermute(b_high, "y", down)
    p0 = jnp.stack([w_0, w_1, w_2, w_3])
    p1 = lax.ppermute(p0, "zh", pair)
    p2 = lax.ppermute(p0, "c", pair)
    p3 = lax.ppermute(p1, "c", pair)
    a_own = jnp.stack([x_own, proj_left[0]])
    a_prev = lax.ppermute(a_own, "y", up)
    a_after = lax.ppermute(a_own, "y", down)
    x_cut = a_prev[0]
    l_cut = a_after[1]
    x_far = lax.ppermute(x_cut, "y", up)
    l_far = lax.ppermute(l_cut, "y", down)

    bulk_rows = (bulk_second, b_prev, b_after, b_low, b_high)
    bulk_parts = bulk_bond(meta, h, *bulk_rows, q0, b_own, q1, q2, q3)
    left, left_down, left_up, left_far, right_own, right_send = window_bonds(
        meta, h, a_own, a_prev, a_after, x_far, l_far, p0, p1, p2, p3, *bulk_rows, b_own, q1, q2, q3,
        *bulk_parts,
    )
    got = lax.ppermute(right_send, "c", pair)
    left_down = lax.ppermute(left_down, "y", down)
    left_up = lax.ppermute(left_up, "y", up)
    left_far = lax.ppermute(left_far, "y", across)
    right = (right_own + got).astype(BF16)
    got = exchange(right, ("zh", "y"))
    left = sum(v.astype(F32) for v in (left, left_down, left_up, left_far))
    bulk_left = left[:, 2 * width :]
    left = left[:, : 2 * width] * jnp.concatenate([keep_left, keep_left])
    left = left.astype(BF16)
    returned = lax.ppermute(left, SITE, back)
    ends = bulk_ends(bulk_left, got)
    ends = exchange(ends, SITE)
    new_sites = join(meta, got, returned)
    new_first, new_second = spread(ends)
    return new_sites, new_first, new_second


def solution(mesh):
    finer = Mesh(mesh.devices.reshape(4, 2, 2, 4, 2), SITE + BOND)
    rows = P(BOND, None)
    stacked = P(SITE, BOND, None)
    placed = (stacked,) * 3 + (rows,) * 5 + (P(), P(SITE), P(SITE))
    return jax.shard_map(
        half_step,
        mesh=finer,
        in_specs=placed,
        out_specs=(stacked, rows, rows),
        check_vma=False,
    )
```

```python
import jax
import jax.numpy as jnp
from jax import lax
from jax.experimental import pallas as pl
from jax.experimental.pallas import tpu as pltpu
from jax.sharding import Mesh
from jax.sharding import PartitionSpec as P


SITE = ("x", "zl")
BOND = ("zh", "y", "c")
VMEM_BYTES = 18 * 1024 * 1024
F32 = jnp.float32
BF16 = jnp.bfloat16


def dot(a, b, dims):
    return lax.dot_general(a, b, (dims, ((), ())), preferred_element_type=F32)


def split_kernel(
    site, edge, proj, bulk, bulk_proj, bulk_left, w_0, w_1, w_2, w_3, b_0, b_1, b_2, b_3
):
    me = lax.axis_index("y")
    g = 2 * lax.axis_index("x") + lax.axis_index("zl")
    quarter, width = 256, 1024
    column = lax.broadcasted_iota(jnp.int32, (width, 128), 1)
    source = (column // 8) * 64 + g * 8 + column % 8
    chosen = jnp.where(lax.broadcasted_iota(jnp.int32, (width, 128), 0) == source, 1.0, 0.0)
    chosen = chosen.astype(BF16)
    for s in range(2):
        part = dot(bulk_left[:, s * width : (s + 1) * width], chosen, ((1,), (0,))).astype(BF16)
        for ref in (b_0, b_1, b_2, b_3):
            ref[:, width + s * 128 : width + (s + 1) * 128] = part
    for step, w_ref, b_ref in ((0, w_0, b_0), (1, w_1, b_1), (3, w_2, b_2), (2, w_3, b_3)):
        q = lax.rem(me + step, 4)
        for t in range(2):
            cols = pl.ds(pl.multiple_of(t * width + q * quarter, quarter), quarter)
            low = slice(t * quarter, (t + 1) * quarter)
            high = slice((2 + t) * quarter, (3 + t) * quarter)
            w_ref[:, low] = site[0, :, cols]
            b_ref[:, low] = bulk[:, cols]
            w_ref[:, high] = jnp.where(g == 0, edge[:, cols], proj[0, :, cols])
            b_ref[:, high] = bulk_proj[:, cols]


def split(sites, edge, proj, bulk, bulk_proj, bulk_left):
    one = pl.BlockSpec((1, 64, 2048), lambda i: (0, 0, 0))
    flat = pl.BlockSpec((64, 2048), lambda i: (0, 0))
    return pl.pallas_call(
        split_kernel,
        grid=(1,),
        out_shape=(jax.ShapeDtypeStruct((64, 1024), BF16),) * 4
        + (jax.ShapeDtypeStruct((64, 1280), BF16),) * 4,
        in_specs=[one, flat, one, flat, flat, flat],
        out_specs=(pl.BlockSpec((64, 1024), lambda i: (0, 0)),) * 4
        + (pl.BlockSpec((64, 1280), lambda i: (0, 0)),) * 4,
        cost_estimate=pl.CostEstimate(
            flops=40_000_000, bytes_accessed=3_000_000, transcendentals=0
        ),
        name="split",
    )(sites, edge, proj, bulk, bulk_proj, bulk_left)


def theta(h, base, x_of, y_part, raw, out):
    for s0 in range(2):
        raw[s0] = dot(x_of(s0), y_part, ((1,), (0,)))
    step, half = 32, 256

    def chunk(i, _):
        r = pl.ds(pl.multiple_of(i * step, step), step)
        parts = [raw[k // 2, r, (k % 2) * half : (k % 2 + 1) * half] for k in range(4)]
        for s in range(2):
            for t in range(2):
                row = base + 4 * (2 * s + t)
                val = h[row] * parts[0]
                for k in range(1, 4):
                    val = val + h[row + k] * parts[k]
                out[s, r, t * half : (t + 1) * half] = val.astype(out.dtype)
        return 0

    lax.fori_loop(0, 256 // step, chunk, 0, unroll=True)


def row_copies(parts, low, high, ys, zh, c, me, sem):
    copies = []
    for n, part in enumerate(parts):
        z_of = lax.rem(zh + n % 2, 2)
        c_of = lax.rem(c + n // 2, 2)
        for y, step in enumerate((0, 3, 1, 2)):
            at = pl.multiple_of((z_of * 8 + lax.rem(me + step, 4) * 2 + c_of) * 64, 64)
            copies.append(
                pltpu.make_async_copy(
                    part.at[y, :, low:high], ys.at[pl.ds(at, 64), :], sem.at[n * 4 + y]
                )
            )
    return copies


def bulk_kernel(
    meta, h, own, prev, after, far_low, far_high, l_parts, b0, b1, b2, b3,
    left_ref, keep_ref, send_ref, xs, ys, rs, ls, raw, th, tmp, sem, sem_y,
):
    c, zh, me, g = meta[0], meta[1], meta[2], meta[4]
    ny, block, width, cols = 4, 64, 1024, 512
    copies = row_copies((b0, b1, b2, b3), 0, cols, ys, zh, c, me, sem_y)
    for n, part in enumerate((b0, b1, b2, b3)):
        to = rs.at[n % 2, pl.ds(pl.multiple_of(lax.rem(c + n // 2, 2) * block, block), block), :]
        copies.append(pltpu.make_async_copy(part.at[ny], to, sem.at[6 + n]))
    for n, part in enumerate((own, prev, after)):
        copies.append(pltpu.make_async_copy(part, xs.at[n * block : (n + 1) * block, :], sem.at[n]))
    last = slice(3 * block, 4 * block)
    copies.append(pltpu.make_async_copy(far_low, xs.at[last, 0:width], sem.at[3]))
    copies.append(pltpu.make_async_copy(far_high, xs.at[last, width : 2 * width], sem.at[4]))
    copies.append(pltpu.make_async_copy(l_parts.at[:, :, width : width + 256], ls, sem.at[5]))
    for copy in copies:
        copy.start()
    for copy in copies:
        copy.wait()

    theta(h, 32, lambda s: xs[:, s * width : (s + 1) * width], ys[...], raw, th)
    far = lax.rem(lax.div(g, ny) + zh, 2)
    part = None
    for s in range(2):
        here = th[s].astype(BF16)
        left = dot(here, rs[far], ((1,), (1,))).astype(BF16)
        for j in range(ny):
            left_ref[j, :, s * 128 : (s + 1) * 128] = left[j * block : (j + 1) * block]
        for j in range(ny):
            l_part = ls[j, :, s * 128 : (s + 1) * 128]
            one = dot(l_part, here[j * block : (j + 1) * block], ((0,), (0,)))
            part = one if part is None else part + one
    tmp[...] = part
    for at in range(2 * ny):
        mine = pl.multiple_of(at * 16 + c * 8, 8)
        other = pl.multiple_of(at * 16 + (1 - c) * 8, 8)
        keep_ref[at] = tmp[pl.ds(mine, 8), :]
        send_ref[at] = tmp[pl.ds(other, 8), :]


def window_kernel(
    meta, h, a_own, a_prev, a_after, x_far, l_far, p0, p1, p2, p3, own, prev, after, far_low, far_high,
    b0, b1, b2, b3, bulk_left, bulk_keep, bulk_send, left_0, left_1, left_2, left_3, keep_out, send_out,
    xs, ls, xb, ys, yb, raw, th, tmp, left, keep_rows, send_rows, sem, sem_y, sem_r, sem_b, sem_out,
):
    c, zh, me, first = meta[0], meta[1], meta[2], meta[3]
    ny, block, width, cols = 4, 64, 1024, 512
    rows = [slice(n * block, (n + 1) * block) for n in range(ny)]
    early = [
        pltpu.make_async_copy(part, xs.at[rows[n], :], sem.at[n])
        for n, part in enumerate((a_own.at[0], a_prev.at[0], a_after.at[0], x_far))
    ]
    early += row_copies((p0, p1, p2, p3), 0, cols, ys.at[:, 0:cols], zh, c, me, sem_y)
    edge = row_copies((b0, b1, b2, b3), 0, cols, yb, zh, c, me, sem_b)
    proj = row_copies((p0, p1, p2, p3), cols, 2 * cols, ys.at[:, cols : 2 * cols], zh, c, me, sem_r)
    bulk = [
        pltpu.make_async_copy(part, xb.at[rows[n], :], sem.at[4 + n])
        for n, part in enumerate((own, prev, after))
    ]
    bulk.append(pltpu.make_async_copy(far_low, xb.at[rows[3], 0:width], sem.at[7]))
    bulk.append(pltpu.make_async_copy(far_high, xb.at[rows[3], width : 2 * width], sem.at[8]))
    late = [
        pltpu.make_async_copy(part, ls.at[rows[n], :], sem.at[9 + n])
        for n, part in enumerate((a_own.at[1], a_prev.at[1], a_after.at[1], l_far))
    ]
    late.append(pltpu.make_async_copy(bulk_keep, keep_rows.at[:, block : block + 8, :], sem.at[13]))
    late.append(pltpu.make_async_copy(bulk_send, send_rows.at[:, block : block + 8, :], sem.at[14]))
    for n in range(ny):
        proj.append(
            pltpu.make_async_copy(
                bulk_left.at[n], left.at[rows[n], 2 * width : 2 * width + 256], sem.at[15 + n]
            )
        )
    for copy in early:
        copy.start()

    @pl.when(first == 1)
    def _():
        for copy in edge:
            copy.start()

    for copy in proj:
        copy.start()

    @pl.when(first == 1)
    def _():
        for copy in bulk:
            copy.start()

    for copy in late:
        copy.start()
    for copy in early:
        copy.wait()

    @pl.when(first == 1)
    def _():
        for copy in edge:
            copy.wait()
        theta(h, 0, lambda s: xs[:, s * width : (s + 1) * width], yb[...], raw, th)

    @pl.when(first == 0)
    def _():
        theta(h, 0, lambda s: xs[:, s * width : (s + 1) * width], ys[:, 0:cols], raw, th)

    for copy in proj:
        copy.wait()

    def left_chunk(n, _):
        k_at = pl.multiple_of(n * 256, 256)
        r_part = ys[pl.ds(k_at, 256), cols : 2 * cols]
        for s in range(2):
            lanes = pl.ds(pl.multiple_of(s * width + n * 256, 256), 256)
            left[:, lanes] = dot(th[s], r_part, ((1,), (1,))).astype(BF16)
        return 0

    lax.fori_loop(0, 4, left_chunk, 0, unroll=True)
    outs = [
        pltpu.make_async_copy(left.at[rows[n], :], ref, sem_out.at[n])
        for n, ref in enumerate((left_0, left_1, left_2, left_3))
    ]
    for copy in outs:
        copy.start()

    @pl.when(first == 1)
    def _():
        for copy in bulk:
            copy.wait()
        theta(h, 16, lambda s: xb[:, s * width : (s + 1) * width], ys[:, 0:cols], raw, th)

    for copy in late:
        copy.wait()

    def right_chunk(n, _):
        part = None
        for s in range(2):
            l_part = ls[:, pl.ds(pl.multiple_of(s * width + n * 256, 256), 256)]
            one = dot(l_part, th[s], ((0,), (0,)))
            part = one if s == 0 else part + one
        tmp[...] = part
        for j in range(2):
            mine = pl.multiple_of(j * 128 + c * block, block)
            other = pl.multiple_of(j * 128 + (1 - c) * block, block)
            keep_rows[2 * n + j, 0:block, :] = tmp[pl.ds(mine, block), :]
            send_rows[2 * n + j, 0:block, :] = tmp[pl.ds(other, block), :]
        return 0

    lax.fori_loop(0, 4, right_chunk, 0, unroll=True)
    outs.append(pltpu.make_async_copy(send_rows, send_out, sem_out.at[4]))
    outs.append(pltpu.make_async_copy(keep_rows, keep_out, sem_out.at[5]))
    for copy in outs[4:]:
        copy.start()
    for copy in outs:
        copy.wait()


def call(kernel, outs, out_space, scratch, flops, meta, h, *arrays):
    smem = pl.BlockSpec(memory_space=pltpu.SMEM)
    anywhere = pl.BlockSpec(memory_space=pltpu.HBM)
    return pl.pallas_call(
        kernel,
        out_shape=outs,
        in_specs=[smem, smem] + [anywhere] * len(arrays),
        out_specs=(pl.BlockSpec(memory_space=out_space),) * len(outs),
        scratch_shapes=scratch,
        compiler_params=pltpu.CompilerParams(vmem_limit_bytes=VMEM_BYTES),
        cost_estimate=pl.CostEstimate(
            flops=flops, bytes_accessed=10_000_000, transcendentals=0
        ),
    )(meta, h, *arrays)


def ends_kernel(left, got, out):
    rights = [got[q].astype(F32) + got[4 + q].astype(F32) for q in range(4)]
    rights = [rights[q][:, t * 256 : (t + 1) * 256] for t in range(2) for q in range(4)]
    rights = jnp.concatenate(rights, axis=0).astype(BF16)
    lefts = left[...].astype(BF16)
    for g in range(8):
        out[g, :, 0:256] = lefts
        out[g, :, 256:512] = rights


def bulk_ends(left, got):
    return pl.pallas_call(
        ends_kernel,
        grid=(1,),
        in_specs=[
            pl.BlockSpec((64, 256), lambda i: (0, 0)),
            pl.BlockSpec((8, 8, 512), lambda i: (0, 8, 0)),
        ],
        out_specs=pl.BlockSpec((8, 64, 512), lambda i: (0, 0, 0)),
        out_shape=jax.ShapeDtypeStruct((8, 64, 512), BF16),
        cost_estimate=pl.CostEstimate(flops=1_000_000, bytes_accessed=700_000, transcendentals=0),
        compiler_params=pltpu.CompilerParams(vmem_limit_bytes=8 * 1024 * 1024),
        name="finish",
    )(left, got)


def spread_kernel(ends, first, second):
    for g in range(8):
        for s in range(2):
            second[:, s * 1024 + g * 128 : s * 1024 + (g + 1) * 128] = ends[
                g, :, s * 128 : (s + 1) * 128
            ]
    for pair in range(4):
        rows = []
        for g in (2 * pair, 2 * pair + 1):
            right = ends[g, :, 256:512].astype(F32)
            rows.append(jnp.concatenate([right[8 * k : 8 * (k + 1)] for k in range(8)], axis=1))
        first[16 * pair : 16 * (pair + 1), :] = jnp.concatenate(rows, axis=0).astype(BF16)


def spread(ends):
    rows = jax.ShapeDtypeStruct((64, 2048), BF16)
    return pl.pallas_call(
        spread_kernel,
        out_shape=(rows, rows),
        cost_estimate=pl.CostEstimate(flops=1_000_000, bytes_accessed=1_000_000, transcendentals=0),
        compiler_params=pltpu.CompilerParams(vmem_limit_bytes=8 * 1024 * 1024),
        name="spread",
    )(ends)


def bulk_bond(meta, h, *arrays):
    sums = jax.ShapeDtypeStruct((8, 8, 512), F32)
    return call(
        bulk_kernel,
        (jax.ShapeDtypeStruct((4, 64, 256), BF16), sums, sums),
        pltpu.VMEM,
        [
            pltpu.VMEM((256, 2048), BF16),
            pltpu.VMEM((1024, 512), BF16),
            pltpu.VMEM((2, 128, 512), BF16),
            pltpu.VMEM((4, 64, 256), BF16),
            pltpu.VMEM((2, 256, 512), F32),
            pltpu.VMEM((2, 256, 512), F32),
            pltpu.VMEM((128, 512), F32),
            pltpu.SemaphoreType.DMA((10,)),
            pltpu.SemaphoreType.DMA((16,)),
        ],
        1_000_000_000,
        meta,
        h,
        *arrays,
    )


def window_bonds(meta, h, *arrays):
    rows = jax.ShapeDtypeStruct((64, 2304), BF16)
    sums = jax.ShapeDtypeStruct((8, 72, 512), F32)
    return call(
        window_kernel,
        (rows, rows, rows, rows, sums, sums),
        pltpu.HBM,
        [
            pltpu.VMEM((256, 2048), BF16),
            pltpu.VMEM((256, 2048), BF16),
            pltpu.VMEM((256, 2048), BF16),
            pltpu.VMEM((1024, 1024), BF16),
            pltpu.VMEM((1024, 512), BF16),
            pltpu.VMEM((2, 256, 512), F32),
            pltpu.VMEM((2, 256, 512), BF16),
            pltpu.VMEM((256, 512), F32),
            pltpu.VMEM((256, 2304), BF16),
            pltpu.VMEM((8, 72, 512), F32),
            pltpu.VMEM((8, 72, 512), F32),
            pltpu.SemaphoreType.DMA((19,)),
            pltpu.SemaphoreType.DMA((16,)),
            pltpu.SemaphoreType.DMA((16,)),
            pltpu.SemaphoreType.DMA((16,)),
            pltpu.SemaphoreType.DMA((6,)),
        ],
        3_000_000_000,
        meta,
        h,
        *arrays,
    )


def join_kernel(meta, got, returned, out):
    row = lax.broadcasted_iota(jnp.int32, (64, 1), 0) + meta[5] * 64
    keep = jnp.where(row < meta[6], 1.0, 0.0).astype(F32)
    for q in range(4):
        part = (got[q, 0:64].astype(F32) + got[4 + q, 0:64].astype(F32)) * keep
        for t in range(2):
            at = t * 1024 + q * 256
            out[0, :, at : at + 256] = part[:, t * 256 : (t + 1) * 256].astype(BF16)
    out[1] = returned[...]


def join(meta, got, returned):
    vmem = pl.BlockSpec(memory_space=pltpu.VMEM)
    return pl.pallas_call(
        join_kernel,
        out_shape=jax.ShapeDtypeStruct((2, 64, 2048), BF16),
        in_specs=[pl.BlockSpec(memory_space=pltpu.SMEM), vmem, vmem],
        out_specs=vmem,
        cost_estimate=pl.CostEstimate(flops=1_000_000, bytes_accessed=1_300_000, transcendentals=0),
        compiler_params=pltpu.CompilerParams(vmem_limit_bytes=8 * 1024 * 1024),
        name="join",
    )(meta, got, returned)


def half_step(
    sites,
    proj_left,
    proj_right,
    edge_right,
    bulk_first,
    bulk_second,
    bulk_left_proj,
    bulk_right_proj,
    gate,
    gate_mask,
    bond_dims,
):
    width = sites.shape[2] // 2
    groups = lax.axis_size(SITE)
    ny = lax.axis_size("y")
    here = lax.axis_index(SITE)
    zh, y, c = (lax.axis_index(name) for name in BOND)
    first_group = here == 0
    identity = jnp.eye(4, dtype=F32)
    weight = gate_mask[0].astype(F32)
    mixer = weight * gate + (1.0 - weight) * identity
    mixer_left = jnp.where(first_group, gate, mixer)
    positions = jnp.arange(width, dtype=jnp.int32)
    keep = (positions < bond_dims[0]).astype(F32)
    keep_left = jnp.where(first_group, 1.0, keep)
    around = [(g, (g + 1) % groups) for g in range(groups)]

    meta = jnp.stack(
        [c, zh, y, first_group.astype(jnp.int32), here, lax.axis_index(BOND), bond_dims[0]]
    ).astype(jnp.int32)
    h = jnp.concatenate([mixer_left.reshape(16), mixer.reshape(16), gate.reshape(16)])
    up = [(k, (k + 1) % ny) for k in range(ny)]
    down = [(b, a) for a, b in up]
    back = [(b, a) for a, b in around]

    def exchange(v, axis):
        return lax.all_to_all(v, axis, split_axis=0, concat_axis=0, tiled=True)

    pair = [(0, 1), (1, 0)]

    x_own = lax.ppermute(sites[sites.shape[0] - 1], SITE, around)
    b_prev = lax.ppermute(bulk_second, "y", up)
    b_after = lax.ppermute(bulk_second, "y", down)

    across = [(k, (k + 2) % ny) for k in range(ny)]
    w_0, w_1, w_2, w_3, b_0, b_1, b_2, b_3 = split(
        sites, edge_right, proj_right, bulk_first, bulk_right_proj, bulk_left_proj
    )
    b_1 = lax.ppermute(b_1, "y", up)
    b_2 = lax.ppermute(b_2, "y", down)
    b_3 = lax.ppermute(b_3, "y", across)
    w_1 = lax.ppermute(w_1, "y", up)
    w_2 = lax.ppermute(w_2, "y", down)
    w_3 = lax.ppermute(w_3, "y", across)
    q0 = jnp.stack([b_0, b_1, b_2, b_3])
    step = lax.rem(here + 2 * ny - y, ny)
    place = jnp.where(step == 0, 0, jnp.where(step == 3, 1, step + 1))
    chosen = lax.dynamic_index_in_dim(q0, place, 0)[:, :, width // 2 : width]
    b_own = jnp.concatenate([q0[:, :, : width // 2], chosen], axis=0)
    q1 = lax.ppermute(b_own, "zh", pair)
    q2 = lax.ppermute(b_own, "c", pair)
    q3 = lax.ppermute(q1, "c", pair)
    b_low = b_prev[:, :width]
    b_high = b_after[:, width:]
    b_low = lax.ppermute(b_low, "y", up)
    b_high = lax.ppermute(b_high, "y", down)
    p0 = jnp.stack([w_0, w_1, w_2, w_3])
    p1 = lax.ppermute(p0, "zh", pair)
    p2 = lax.ppermute(p0, "c", pair)
    p3 = lax.ppermute(p1, "c", pair)
    a_own = jnp.stack([x_own, proj_left[0]])
    a_prev = lax.ppermute(a_own, "y", up)
    a_after = lax.ppermute(a_own, "y", down)
    x_cut = a_prev[0]
    l_cut = a_after[1]
    x_far = lax.ppermute(x_cut, "y", up)
    l_far = lax.ppermute(l_cut, "y", down)

    bulk_rows = (bulk_second, b_prev, b_after, b_low, b_high)
    bulk_parts = bulk_bond(meta, h, *bulk_rows, q0, b_own, q1, q2, q3)
    left, left_down, left_up, left_far, right_own, right_send = window_bonds(
        meta, h, a_own, a_prev, a_after, x_far, l_far, p0, p1, p2, p3, *bulk_rows, b_own, q1, q2, q3,
        *bulk_parts,
    )
    got = lax.ppermute(right_send, "c", pair)
    left_down = lax.ppermute(left_down, "y", down)
    left_up = lax.ppermute(left_up, "y", up)
    left_far = lax.ppermute(left_far, "y", across)
    right = (right_own + got).astype(BF16)
    got = exchange(right, ("zh", "y"))
    left = sum(v.astype(F32) for v in (left, left_down, left_up, left_far))
    bulk_left = left[:, 2 * width :]
    left = left[:, : 2 * width] * jnp.concatenate([keep_left, keep_left])
    left = left.astype(BF16)
    returned = lax.ppermute(left, SITE, back)
    ends = bulk_ends(bulk_left, got)
    ends = exchange(ends, SITE)
    new_sites = join(meta, got, returned)
    new_first, new_second = spread(ends)
    return new_sites, new_first, new_second


def solution(mesh):
    finer = Mesh(mesh.devices.reshape(4, 2, 2, 4, 2), SITE + BOND)
    rows = P(BOND, None)
    stacked = P(SITE, BOND, None)
    placed = (stacked,) * 3 + (rows,) * 5 + (P(), P(SITE), P(SITE))
    return jax.shard_map(
        half_step,
        mesh=finer,
        in_specs=placed,
        out_specs=(stacked, rows, rows),
        check_vma=False,
    )
```

```python
import jax
import jax.numpy as jnp
from jax import lax
from jax.experimental import pallas as pl
from jax.experimental.pallas import tpu as pltpu
from jax.sharding import Mesh
from jax.sharding import PartitionSpec as P


SITE = ("x", "zl")
BOND = ("zh", "y", "c")
VMEM_BYTES = 18 * 1024 * 1024
F32 = jnp.float32
BF16 = jnp.bfloat16


def dot(a, b, dims):
    return lax.dot_general(a, b, (dims, ((), ())), preferred_element_type=F32)


def split_kernel(
    site, edge, proj, bulk, bulk_proj, bulk_left, w_0, w_1, w_2, w_3, b_0, b_1, b_2, b_3
):
    me = lax.axis_index("y")
    g = 2 * lax.axis_index("x") + lax.axis_index("zl")
    quarter, width = 256, 1024
    column = lax.broadcasted_iota(jnp.int32, (width, 128), 1)
    source = (column // 8) * 64 + g * 8 + column % 8
    chosen = jnp.where(lax.broadcasted_iota(jnp.int32, (width, 128), 0) == source, 1.0, 0.0)
    chosen = chosen.astype(BF16)
    for s in range(2):
        part = dot(bulk_left[:, s * width : (s + 1) * width], chosen, ((1,), (0,))).astype(BF16)
        for ref in (b_0, b_1, b_2, b_3):
            ref[:, width + s * 128 : width + (s + 1) * 128] = part
    for step, w_ref, b_ref in ((0, w_0, b_0), (1, w_1, b_1), (3, w_2, b_2), (2, w_3, b_3)):
        q = lax.rem(me + step, 4)
        for t in range(2):
            cols = pl.ds(pl.multiple_of(t * width + q * quarter, quarter), quarter)
            low = slice(t * quarter, (t + 1) * quarter)
            high = slice((2 + t) * quarter, (3 + t) * quarter)
            w_ref[:, low] = site[0, :, cols]
            b_ref[:, low] = bulk[:, cols]
            w_ref[:, high] = jnp.where(g == 0, edge[:, cols], proj[0, :, cols])
            b_ref[:, high] = bulk_proj[:, cols]


def split(sites, edge, proj, bulk, bulk_proj, bulk_left):
    one = pl.BlockSpec((1, 64, 2048), lambda i: (0, 0, 0))
    flat = pl.BlockSpec((64, 2048), lambda i: (0, 0))
    return pl.pallas_call(
        split_kernel,
        grid=(1,),
        out_shape=(jax.ShapeDtypeStruct((64, 1024), BF16),) * 4
        + (jax.ShapeDtypeStruct((64, 1280), BF16),) * 4,
        in_specs=[one, flat, one, flat, flat, flat],
        out_specs=(pl.BlockSpec((64, 1024), lambda i: (0, 0)),) * 4
        + (pl.BlockSpec((64, 1280), lambda i: (0, 0)),) * 4,
        cost_estimate=pl.CostEstimate(
            flops=40_000_000, bytes_accessed=3_000_000, transcendentals=0
        ),
        name="split",
    )(sites, edge, proj, bulk, bulk_proj, bulk_left)


def theta(h, base, x_of, y_part, raw, out):
    for s0 in range(2):
        raw[s0] = dot(x_of(s0), y_part, ((1,), (0,)))
    step, half = 32, 256

    def chunk(i, _):
        r = pl.ds(pl.multiple_of(i * step, step), step)
        parts = [raw[k // 2, r, (k % 2) * half : (k % 2 + 1) * half] for k in range(4)]
        for s in range(2):
            for t in range(2):
                row = base + 4 * (2 * s + t)
                val = h[row] * parts[0]
                for k in range(1, 4):
                    val = val + h[row + k] * parts[k]
                out[s, r, t * half : (t + 1) * half] = val.astype(out.dtype)
        return 0

    lax.fori_loop(0, 256 // step, chunk, 0, unroll=True)


def row_copies(parts, low, high, ys, zh, c, me, sem):
    copies = []
    for n, part in enumerate(parts):
        z_of = lax.rem(zh + n % 2, 2)
        c_of = lax.rem(c + n // 2, 2)
        for y, step in enumerate((0, 3, 1, 2)):
            at = pl.multiple_of((z_of * 8 + lax.rem(me + step, 4) * 2 + c_of) * 64, 64)
            copies.append(
                pltpu.make_async_copy(
                    part.at[y, :, low:high], ys.at[pl.ds(at, 64), :], sem.at[n * 4 + y]
                )
            )
    return copies


def bulk_kernel(
    meta, h, own, prev, after, far_low, far_high, l_parts, b0, b1, b2, b3,
    left_ref, keep_ref, send_ref, xs, ys, rs, ls, raw, th, tmp, sem, sem_y,
):
    c, zh, me, g = meta[0], meta[1], meta[2], meta[4]
    ny, block, width, cols = 4, 64, 1024, 512
    copies = row_copies((b0, b1, b2, b3), 0, cols, ys, zh, c, me, sem_y)
    for n, part in enumerate((b0, b1, b2, b3)):
        to = rs.at[n % 2, pl.ds(pl.multiple_of(lax.rem(c + n // 2, 2) * block, block), block), :]
        copies.append(pltpu.make_async_copy(part.at[ny], to, sem.at[6 + n]))
    for n, part in enumerate((own, prev, after)):
        copies.append(pltpu.make_async_copy(part, xs.at[n * block : (n + 1) * block, :], sem.at[n]))
    last = slice(3 * block, 4 * block)
    copies.append(pltpu.make_async_copy(far_low, xs.at[last, 0:width], sem.at[3]))
    copies.append(pltpu.make_async_copy(far_high, xs.at[last, width : 2 * width], sem.at[4]))
    copies.append(pltpu.make_async_copy(l_parts.at[:, :, width : width + 256], ls, sem.at[5]))
    for copy in copies:
        copy.start()
    for copy in copies:
        copy.wait()

    theta(h, 32, lambda s: xs[:, s * width : (s + 1) * width], ys[...], raw, th)
    far = lax.rem(lax.div(g, ny) + zh, 2)
    part = None
    for s in range(2):
        here = th[s].astype(BF16)
        left = dot(here, rs[far], ((1,), (1,))).astype(BF16)
        for j in range(ny):
            left_ref[j, :, s * 128 : (s + 1) * 128] = left[j * block : (j + 1) * block]
        for j in range(ny):
            l_part = ls[j, :, s * 128 : (s + 1) * 128]
            one = dot(l_part, here[j * block : (j + 1) * block], ((0,), (0,)))
            part = one if part is None else part + one
    tmp[...] = part
    for at in range(2 * ny):
        mine = pl.multiple_of(at * 16 + c * 8, 8)
        other = pl.multiple_of(at * 16 + (1 - c) * 8, 8)
        keep_ref[at] = tmp[pl.ds(mine, 8), :]
        send_ref[at] = tmp[pl.ds(other, 8), :]


def window_kernel(
    meta, h, a_own, a_prev, a_after, x_far, l_far, p0, p1, p2, p3, own, prev, after, far_low, far_high,
    b0, b1, b2, b3, bulk_left, bulk_keep, bulk_send, left_0, left_1, left_2, left_3, keep_rows, send_rows,
    xs, ls, xb, ys, yb, raw, th, tmp, sem, sem_y, sem_r, sem_b,
):
    c, zh, me, first = meta[0], meta[1], meta[2], meta[3]
    ny, block, width, cols = 4, 64, 1024, 512
    rows = [slice(n * block, (n + 1) * block) for n in range(ny)]
    early = [
        pltpu.make_async_copy(part, xs.at[rows[n], :], sem.at[n])
        for n, part in enumerate((a_own.at[0], a_prev.at[0], a_after.at[0], x_far))
    ]
    early += row_copies((p0, p1, p2, p3), 0, cols, ys.at[:, 0:cols], zh, c, me, sem_y)
    edge = row_copies((b0, b1, b2, b3), 0, cols, yb, zh, c, me, sem_b)
    proj = row_copies((p0, p1, p2, p3), cols, 2 * cols, ys.at[:, cols : 2 * cols], zh, c, me, sem_r)
    bulk = [
        pltpu.make_async_copy(part, xb.at[rows[n], :], sem.at[4 + n])
        for n, part in enumerate((own, prev, after))
    ]
    bulk.append(pltpu.make_async_copy(far_low, xb.at[rows[3], 0:width], sem.at[7]))
    bulk.append(pltpu.make_async_copy(far_high, xb.at[rows[3], width : 2 * width], sem.at[8]))
    late = [
        pltpu.make_async_copy(part, ls.at[rows[n], :], sem.at[9 + n])
        for n, part in enumerate((a_own.at[1], a_prev.at[1], a_after.at[1], l_far))
    ]
    late.append(pltpu.make_async_copy(bulk_keep, keep_rows.at[:, block : block + 8, :], sem.at[13]))
    late.append(pltpu.make_async_copy(bulk_send, send_rows.at[:, block : block + 8, :], sem.at[14]))
    for n, ref in enumerate((left_0, left_1, left_2, left_3)):
        proj.append(
            pltpu.make_async_copy(
                bulk_left.at[n], ref.at[:, 2 * width : 2 * width + 256], sem.at[15 + n]
            )
        )
    for copy in early:
        copy.start()

    @pl.when(first == 1)
    def _():
        for copy in edge:
            copy.start()

    for copy in proj:
        copy.start()

    @pl.when(first == 1)
    def _():
        for copy in bulk:
            copy.start()

    for copy in late:
        copy.start()
    for copy in early:
        copy.wait()

    @pl.when(first == 1)
    def _():
        for copy in edge:
            copy.wait()
        theta(h, 0, lambda s: xs[:, s * width : (s + 1) * width], yb[...], raw, th)

    @pl.when(first == 0)
    def _():
        theta(h, 0, lambda s: xs[:, s * width : (s + 1) * width], ys[:, 0:cols], raw, th)

    for copy in proj:
        copy.wait()

    def left_chunk(m, _):
        k_at = pl.multiple_of(m * 256, 256)
        r_part = ys[pl.ds(k_at, 256), cols : 2 * cols]
        for s in range(2):
            lanes = pl.ds(pl.multiple_of(s * width + m * 256, 256), 256)
            part = dot(th[s], r_part, ((1,), (1,))).astype(BF16)
            for n, ref in enumerate((left_0, left_1, left_2, left_3)):
                ref[:, lanes] = part[n * block : (n + 1) * block]
        return 0

    lax.fori_loop(0, 4, left_chunk, 0, unroll=True)

    @pl.when(first == 1)
    def _():
        for copy in bulk:
            copy.wait()
        theta(h, 16, lambda s: xb[:, s * width : (s + 1) * width], ys[:, 0:cols], raw, th)

    for copy in late:
        copy.wait()

    def right_chunk(n, _):
        part = None
        for s in range(2):
            l_part = ls[:, pl.ds(pl.multiple_of(s * width + n * 256, 256), 256)]
            one = dot(l_part, th[s], ((0,), (0,)))
            part = one if s == 0 else part + one
        tmp[...] = part
        for j in range(2):
            mine = pl.multiple_of(j * 128 + c * block, block)
            other = pl.multiple_of(j * 128 + (1 - c) * block, block)
            keep_rows[2 * n + j, 0:block, :] = tmp[pl.ds(mine, block), :]
            send_rows[2 * n + j, 0:block, :] = tmp[pl.ds(other, block), :]
        return 0

    lax.fori_loop(0, 4, right_chunk, 0, unroll=True)


def call(kernel, outs, out_space, scratch, flops, meta, h, *arrays):
    smem = pl.BlockSpec(memory_space=pltpu.SMEM)
    anywhere = pl.BlockSpec(memory_space=pltpu.HBM)
    return pl.pallas_call(
        kernel,
        out_shape=outs,
        in_specs=[smem, smem] + [anywhere] * len(arrays),
        out_specs=(pl.BlockSpec(memory_space=out_space),) * len(outs),
        scratch_shapes=scratch,
        compiler_params=pltpu.CompilerParams(vmem_limit_bytes=VMEM_BYTES),
        cost_estimate=pl.CostEstimate(
            flops=flops, bytes_accessed=10_000_000, transcendentals=0
        ),
    )(meta, h, *arrays)


def ends_kernel(left, got, out):
    rights = [got[q].astype(F32) + got[4 + q].astype(F32) for q in range(4)]
    rights = [rights[q][:, t * 256 : (t + 1) * 256] for t in range(2) for q in range(4)]
    rights = jnp.concatenate(rights, axis=0).astype(BF16)
    lefts = left[...].astype(BF16)
    for g in range(8):
        out[g, :, 0:256] = lefts
        out[g, :, 256:512] = rights


def bulk_ends(left, got):
    return pl.pallas_call(
        ends_kernel,
        grid=(1,),
        in_specs=[
            pl.BlockSpec((64, 256), lambda i: (0, 0)),
            pl.BlockSpec((8, 8, 512), lambda i: (0, 8, 0)),
        ],
        out_specs=pl.BlockSpec((8, 64, 512), lambda i: (0, 0, 0)),
        out_shape=jax.ShapeDtypeStruct((8, 64, 512), BF16),
        cost_estimate=pl.CostEstimate(flops=1_000_000, bytes_accessed=700_000, transcendentals=0),
        compiler_params=pltpu.CompilerParams(vmem_limit_bytes=8 * 1024 * 1024),
        name="finish",
    )(left, got)


def spread_kernel(ends, first, second):
    for g in range(8):
        for s in range(2):
            second[:, s * 1024 + g * 128 : s * 1024 + (g + 1) * 128] = ends[
                g, :, s * 128 : (s + 1) * 128
            ]
    for pair in range(4):
        rows = []
        for g in (2 * pair, 2 * pair + 1):
            right = ends[g, :, 256:512].astype(F32)
            rows.append(jnp.concatenate([right[8 * k : 8 * (k + 1)] for k in range(8)], axis=1))
        first[16 * pair : 16 * (pair + 1), :] = jnp.concatenate(rows, axis=0).astype(BF16)


def spread(ends):
    rows = jax.ShapeDtypeStruct((64, 2048), BF16)
    return pl.pallas_call(
        spread_kernel,
        out_shape=(rows, rows),
        cost_estimate=pl.CostEstimate(flops=1_000_000, bytes_accessed=1_000_000, transcendentals=0),
        compiler_params=pltpu.CompilerParams(vmem_limit_bytes=8 * 1024 * 1024),
        name="spread",
    )(ends)


def bulk_bond(meta, h, *arrays):
    sums = jax.ShapeDtypeStruct((8, 8, 512), F32)
    return call(
        bulk_kernel,
        (jax.ShapeDtypeStruct((4, 64, 256), BF16), sums, sums),
        pltpu.VMEM,
        [
            pltpu.VMEM((256, 2048), BF16),
            pltpu.VMEM((1024, 512), BF16),
            pltpu.VMEM((2, 128, 512), BF16),
            pltpu.VMEM((4, 64, 256), BF16),
            pltpu.VMEM((2, 256, 512), F32),
            pltpu.VMEM((2, 256, 512), F32),
            pltpu.VMEM((128, 512), F32),
            pltpu.SemaphoreType.DMA((10,)),
            pltpu.SemaphoreType.DMA((16,)),
        ],
        1_000_000_000,
        meta,
        h,
        *arrays,
    )


def window_bonds(meta, h, *arrays):
    rows = jax.ShapeDtypeStruct((64, 2304), BF16)
    sums = jax.ShapeDtypeStruct((8, 72, 512), F32)
    return call(
        window_kernel,
        (rows, rows, rows, rows, sums, sums),
        pltpu.VMEM,
        [
            pltpu.VMEM((256, 2048), BF16),
            pltpu.VMEM((256, 2048), BF16),
            pltpu.VMEM((256, 2048), BF16),
            pltpu.VMEM((1024, 1024), BF16),
            pltpu.VMEM((1024, 512), BF16),
            pltpu.VMEM((2, 256, 512), F32),
            pltpu.VMEM((2, 256, 512), BF16),
            pltpu.VMEM((256, 512), F32),
            pltpu.SemaphoreType.DMA((19,)),
            pltpu.SemaphoreType.DMA((16,)),
            pltpu.SemaphoreType.DMA((16,)),
            pltpu.SemaphoreType.DMA((16,)),
        ],
        3_000_000_000,
        meta,
        h,
        *arrays,
    )


def join_kernel(meta, got, returned, out):
    row = lax.broadcasted_iota(jnp.int32, (64, 1), 0) + meta[5] * 64
    keep = jnp.where(row < meta[6], 1.0, 0.0).astype(F32)
    for q in range(4):
        part = (got[q, 0:64].astype(F32) + got[4 + q, 0:64].astype(F32)) * keep
        for t in range(2):
            at = t * 1024 + q * 256
            out[0, :, at : at + 256] = part[:, t * 256 : (t + 1) * 256].astype(BF16)
    out[1] = returned[...]


def join(meta, got, returned):
    vmem = pl.BlockSpec(memory_space=pltpu.VMEM)
    return pl.pallas_call(
        join_kernel,
        out_shape=jax.ShapeDtypeStruct((2, 64, 2048), BF16),
        in_specs=[pl.BlockSpec(memory_space=pltpu.SMEM), vmem, vmem],
        out_specs=vmem,
        cost_estimate=pl.CostEstimate(flops=1_000_000, bytes_accessed=1_300_000, transcendentals=0),
        compiler_params=pltpu.CompilerParams(vmem_limit_bytes=8 * 1024 * 1024),
        name="join",
    )(meta, got, returned)


def half_step(
    sites,
    proj_left,
    proj_right,
    edge_right,
    bulk_first,
    bulk_second,
    bulk_left_proj,
    bulk_right_proj,
    gate,
    gate_mask,
    bond_dims,
):
    width = sites.shape[2] // 2
    groups = lax.axis_size(SITE)
    ny = lax.axis_size("y")
    here = lax.axis_index(SITE)
    zh, y, c = (lax.axis_index(name) for name in BOND)
    first_group = here == 0
    identity = jnp.eye(4, dtype=F32)
    weight = gate_mask[0].astype(F32)
    mixer = weight * gate + (1.0 - weight) * identity
    mixer_left = jnp.where(first_group, gate, mixer)
    positions = jnp.arange(width, dtype=jnp.int32)
    keep = (positions < bond_dims[0]).astype(F32)
    keep_left = jnp.where(first_group, 1.0, keep)
    around = [(g, (g + 1) % groups) for g in range(groups)]

    meta = jnp.stack(
        [c, zh, y, first_group.astype(jnp.int32), here, lax.axis_index(BOND), bond_dims[0]]
    ).astype(jnp.int32)
    h = jnp.concatenate([mixer_left.reshape(16), mixer.reshape(16), gate.reshape(16)])
    up = [(k, (k + 1) % ny) for k in range(ny)]
    down = [(b, a) for a, b in up]
    back = [(b, a) for a, b in around]

    def exchange(v, axis):
        return lax.all_to_all(v, axis, split_axis=0, concat_axis=0, tiled=True)

    pair = [(0, 1), (1, 0)]

    x_own = lax.ppermute(sites[sites.shape[0] - 1], SITE, around)
    b_prev = lax.ppermute(bulk_second, "y", up)
    b_after = lax.ppermute(bulk_second, "y", down)

    across = [(k, (k + 2) % ny) for k in range(ny)]
    w_0, w_1, w_2, w_3, b_0, b_1, b_2, b_3 = split(
        sites, edge_right, proj_right, bulk_first, bulk_right_proj, bulk_left_proj
    )
    b_1 = lax.ppermute(b_1, "y", up)
    b_2 = lax.ppermute(b_2, "y", down)
    b_3 = lax.ppermute(b_3, "y", across)
    w_1 = lax.ppermute(w_1, "y", up)
    w_2 = lax.ppermute(w_2, "y", down)
    w_3 = lax.ppermute(w_3, "y", across)
    q0 = jnp.stack([b_0, b_1, b_2, b_3])
    step = lax.rem(here + 2 * ny - y, ny)
    place = jnp.where(step == 0, 0, jnp.where(step == 3, 1, step + 1))
    chosen = lax.dynamic_index_in_dim(q0, place, 0)[:, :, width // 2 : width]
    b_own = jnp.concatenate([q0[:, :, : width // 2], chosen], axis=0)
    q1 = lax.ppermute(b_own, "zh", pair)
    q2 = lax.ppermute(b_own, "c", pair)
    q3 = lax.ppermute(q1, "c", pair)
    b_low = b_prev[:, :width]
    b_high = b_after[:, width:]
    b_low = lax.ppermute(b_low, "y", up)
    b_high = lax.ppermute(b_high, "y", down)
    p0 = jnp.stack([w_0, w_1, w_2, w_3])
    p1 = lax.ppermute(p0, "zh", pair)
    p2 = lax.ppermute(p0, "c", pair)
    p3 = lax.ppermute(p1, "c", pair)
    a_own = jnp.stack([x_own, proj_left[0]])
    a_prev = lax.ppermute(a_own, "y", up)
    a_after = lax.ppermute(a_own, "y", down)
    x_cut = a_prev[0]
    l_cut = a_after[1]
    x_far = lax.ppermute(x_cut, "y", up)
    l_far = lax.ppermute(l_cut, "y", down)

    bulk_rows = (bulk_second, b_prev, b_after, b_low, b_high)
    bulk_parts = bulk_bond(meta, h, *bulk_rows, q0, b_own, q1, q2, q3)
    left, left_down, left_up, left_far, right_own, right_send = window_bonds(
        meta, h, a_own, a_prev, a_after, x_far, l_far, p0, p1, p2, p3, *bulk_rows, b_own, q1, q2, q3,
        *bulk_parts,
    )
    got = lax.ppermute(right_send, "c", pair)
    left_down = lax.ppermute(left_down, "y", down)
    left_up = lax.ppermute(left_up, "y", up)
    left_far = lax.ppermute(left_far, "y", across)
    right = (right_own + got).astype(BF16)
    got = exchange(right, ("zh", "y"))
    left = sum(v.astype(F32) for v in (left, left_down, left_up, left_far))
    bulk_left = left[:, 2 * width :]
    left = left[:, : 2 * width] * jnp.concatenate([keep_left, keep_left])
    left = left.astype(BF16)
    returned = lax.ppermute(left, SITE, back)
    ends = bulk_ends(bulk_left, got)
    ends = exchange(ends, SITE)
    new_sites = join(meta, got, returned)
    new_first, new_second = spread(ends)
    return new_sites, new_first, new_second


def solution(mesh):
    finer = Mesh(mesh.devices.reshape(4, 2, 2, 4, 2), SITE + BOND)
    rows = P(BOND, None)
    stacked = P(SITE, BOND, None)
    placed = (stacked,) * 3 + (rows,) * 5 + (P(), P(SITE), P(SITE))
    return jax.shard_map(
        half_step,
        mesh=finer,
        in_specs=placed,
        out_specs=(stacked, rows, rows),
        check_vma=False,
    )
```
